32 devices in a mesh: dp: 8 (over z, y), space: 4 (over x, core).
Axes of the slice: x: 2, y: 2, z: 4, core: 2. Of those that a mesh axis runs over, the one named last changes fastest.
Arguments:
- section_three: bfloat16 [8, 16, 32, 768], P('dp', 'space'), may hold values from -6 to 6
- dw_kernel: float32 [7, 7, 768], replicated, may hold values from -0.875 to 0.875
- dw_bias: float32 [768], replicated, may hold values from -3 to 3
- mix_gain: float32 [768], replicated, may hold values from 0.1 to 1.9
- w_expand: bfloat16 [768, 1536], replicated, may hold values from -0.21875 to 0.21875
- w_reduce: bfloat16 [1536, 768], replicated, may hold values from -0.15625 to 0.15625
- layer_scale: float32 [768], replicated, may hold values from 0.3 to 1.5
- down_gain: float32 [768], replicated, may hold values from 0.1 to 1.9
- w_down: bfloat16 [3072, 1536], P(None, 'space'), may hold values from -0.109375 to 0.109375
- owner_table: int32 [8, 128, 1], P('dp'), may hold values from 0 to 7; in each aligned block of 128 rows (0 to 127, 128 to 255, ..., all dimensions but the last counted through in order) at most 16 rows name the same one
- grad_packed: bfloat16 [8, 128, 1536], P('dp', None, 'space'), may hold values from -6 to 6
Outputs:
- packed_tokens: bfloat16 [8, 128, 1536], P('dp', None, 'space')
- grad_mixed: bfloat16 [8, 16, 32, 768], P('dp', 'space')
The draws below stay inside these ranges and needn't reach their ends.
Inputs may be any that keep to these rules, and one draw needn't show every extreme that they name: `owner_table`: among the 128 tokens of one screenshot no owner is named more than 16 times, a bound that some block reaches.
All inputs are finite; a program needn't handle non-finite values.
Results may differ from the reference program's by a relative error of at most 0.018.
Values may be sent and summed in bfloat16 or wider, within the bound.
No kernel may reach another device: no remote copies, remote signals or barrier semaphores. Data moves between devices by JAX's collectives and lax.ppermute only.
A program may use at most 64 MiB of HBM per device.

```python
import math
import jax
import jax.numpy as jnp
import numpy as np
from jax import lax

C3 = 768
C4 = 1536
HID = 1536
KS = 7
H3 = 16
W3 = 32
TILES = 128
CAP = 16
SLOTS = 128
N_DP = 8
N_SPACE = 4


def shard_levels(stream_key, extent, pieces, least, largest):
    def one(axis_at, parts):
        heights = jax.random.uniform(jax.random.fold_in(jax.random.fold_in(stream_key, 6), axis_at), (parts,), jnp.float32, least / len(pieces), largest / len(pieces))
        return jnp.repeat(jnp.exp(heights), extent[axis_at] // parts).reshape((-1,) + (1,) * (len(extent) - axis_at - 1))

    level = one(*pieces[0])
    for cut in pieces[1:]:
        level = level * one(*cut)
    return level


def shared_out(key, own, number, rows, amount, top, bound, lean):
    order = jax.random.permutation(key, amount)
    crowded, usual = portions_of(amount, rows * top, bound, lean, True), portions_of(amount, rows * top, bound, lean, False)
    places = jnp.arange(amount)

    def named(tallies, rotation):
        used = int((tallies > 0).sum())
        fixed = max(1, used // 4)
        moved = fixed + (places - fixed + rotation * (used - fixed)) % max(1, amount - fixed)
        return jnp.zeros((amount,), jnp.int32).at[order[jnp.where(places < fixed, places, moved)]].set(jnp.asarray(tallies, jnp.int32))

    tallies = jnp.where(number % 4 == 0, named(crowded, number // 4), named(usual, number - number // 4 - 1))
    mixed = jax.random.permutation(jax.random.fold_in(own, 3), amount)
    giver, receiver = mixed[0:amount // 2 * 2:2], mixed[1:amount // 2 * 2:2]
    room = jnp.minimum(tallies[giver] - 1, bound - tallies[receiver]) // 2
    room = jnp.where((giver == order[0]) | (receiver == order[0]) | (tallies[receiver] == 0), 0, jnp.maximum(room, 0))
    moved = jax.random.randint(jax.random.fold_in(own, 4), (amount // 2,), 0, 1 << 20) % (room + 1)
    tallies = tallies.at[giver].add(-moved).at[receiver].add(moved)
    labels = jnp.searchsorted(jnp.cumsum(tallies), jnp.arange(rows * top), side="right").astype(jnp.int32)
    table = labels.reshape(top, rows).T
    table = table[jax.random.permutation(jax.random.fold_in(own, 1), rows)]
    rotation = jax.random.randint(jax.random.fold_in(own, 2), (rows, 1), 0, top)
    return jnp.take_along_axis(table, (jnp.arange(top)[None, :] + rotation) % top, axis=1)


def portions_of(amount, total, most, slope, full):
    weights = [(1 << 20) // math.isqrt(grade ** slope) + 1 for grade in range(1, amount + 1)]
    largest = most if full else min(most, max(-(-total // amount), total * weights[0] // sum(weights)))
    least = 1 if total - largest >= amount - 1 else 0
    given, spare = [largest] + [least] * (amount - 1), total - largest - least * (amount - 1)
    while spare > 0:
        candidates = [i for i in range(1, amount) if given[i] < largest] or [i for i in range(1, amount) if given[i] < most]
        pool, budget = sum([weights[i] for i in candidates]), spare
        for i in candidates:
            addition = min(most - given[i], max(1, budget * weights[i] // pool), spare)
            given[i] = given[i] + addition
            spare = spare - addition
    return np.array(given)


def bell_draw(key, shape, spread, most, shards=(), kind=jnp.bfloat16):
    drawn = jax.random.normal(key, shape, jnp.float32) * spread
    if len(shards) > 0:
        drawn = shard_levels(key, shape, shards, -0.22, 0.18) * drawn
    return jnp.clip(drawn, min=-most, max=most).astype(kind)


def setup_inputs(seed: int = 0) -> dict:
    keys = jax.random.split(jax.random.key(seed), 12)
    section_three = bell_draw(keys[0], (N_DP, H3, W3, C3), 1.0, 6.0, ((0, 8), (1, 4)))
    dw_kernel = bell_draw(keys[1], (KS, KS, C3), (KS * KS) ** -0.5, 0.875, (), jnp.float32)
    dw_bias = bell_draw(keys[2], (C3,), 0.5, 3.0, (), jnp.float32)
    mix_gain = jnp.clip(1.0 + 0.18 * jax.random.normal(keys[3], (C3,), jnp.float32), 0.1, 1.9)
    w_expand = bell_draw(keys[4], (C3, HID), C3 ** -0.5, 0.21875)
    w_reduce = bell_draw(keys[5], (HID, C3), HID ** -0.5, 0.15625)
    layer_scale = jnp.clip(jnp.exp(jax.random.uniform(keys[6], (C3,), jnp.float32, math.log(0.3), math.log(1.5))), 0.3, 1.5)
    down_gain = jnp.clip(1.0 + 0.18 * jax.random.normal(keys[7], (C3,), jnp.float32), 0.1, 1.9)
    w_down = bell_draw(keys[8], (4 * C3, C4), (4 * C3) ** -0.5, 0.109375, ((1, 4),))
    owner_table_keys = jax.random.split(jax.random.fold_in(keys[9], 1), N_DP * TILES // TILES)
    owner_table_turns = jax.random.permutation(jax.random.fold_in(keys[9], 3), N_DP * TILES // TILES)
    owner_table = jax.vmap(lambda own, number: shared_out(jax.random.fold_in(keys[9], 2), own, number, TILES, N_DP, 1, CAP, 2))(owner_table_keys, owner_table_turns).reshape((N_DP, TILES, 1))
    grad_packed = bell_draw(keys[10], (N_DP, SLOTS, C4), 1.0, 6.0, ((0, 8), (2, 4)))
    return dict(section_three=section_three, dw_kernel=dw_kernel, dw_bias=dw_bias, mix_gain=mix_gain, w_expand=w_expand, w_reduce=w_reduce, layer_scale=layer_scale, down_gain=down_gain, w_down=w_down, owner_table=owner_table, grad_packed=grad_packed)


def depthwise(padded, kernel, height, width):
    total = jnp.zeros((height, width, kernel.shape[2]), jnp.float32)
    for offset_y in range(KS):
        for offset_x in range(KS):
            total = total + padded[offset_y:offset_y + height, offset_x:offset_x + width] * kernel[offset_y, offset_x]
    return total

def layer_norm(values):
    center = values - lax.optimization_barrier(jnp.mean(values, axis=-1, keepdims=True))
    inv_std = lax.rsqrt(lax.optimization_barrier(jnp.mean(center * center, axis=-1, keepdims=True)) + 1e-06)
    return (center * inv_std, inv_std)

def norm_back(grad, normed, inv_std, gain):
    scaled = grad * gain
    return inv_std * (scaled - lax.optimization_barrier(jnp.mean(scaled, axis=-1, keepdims=True)) - normed * lax.optimization_barrier(jnp.mean(scaled * normed, axis=-1, keepdims=True)))

def gelu_slope(pre):
    cumulative = 0.5 * (1.0 + lax.erf(pre * 0.7071067811865476))
    density = jnp.exp(-0.5 * pre * pre) * 0.3989422804014327
    return cumulative + pre * density

def to_patches(grid):
    height, width, channels = grid.shape
    return grid.reshape(height // 2, 2, width // 2, 2, channels).transpose(0, 2, 1, 3, 4).reshape(height // 2 * (width // 2), 4 * channels)

def from_patches(flat, height, width, channels):
    return flat.reshape(height // 2, width // 2, 2, 2, channels).transpose(0, 2, 1, 3, 4).reshape(height, width, channels)

def slot_ranks(targets):
    onehot = (targets[:, None] == jnp.arange(N_DP, dtype=jnp.int32)[None, :]).astype(jnp.int32)
    earlier = (jnp.cumsum(onehot, axis=0) - onehot).astype(jnp.int32)
    return lax.optimization_barrier(jnp.sum(earlier * onehot, axis=1)).astype(jnp.int32)

def reference(section_three, dw_kernel, dw_bias, mix_gain, w_expand, w_reduce, layer_scale, down_gain, w_down, owner_table, grad_packed):
    half = KS // 2

    def forward_parts(shot):
        padded = jnp.pad(shot.astype(jnp.float32), ((half, half), (half, half), (0, 0)))
        mixed = (depthwise(padded, dw_kernel, H3, W3) + dw_bias).reshape(H3 * W3, C3)
        normed_one, inv_one = layer_norm(mixed)
        first = (normed_one * mix_gain).astype(jnp.bfloat16)
        pre = jnp.dot(first, w_expand, preferred_element_type=jnp.float32)
        hidden = jax.nn.gelu(pre, approximate=False).astype(jnp.bfloat16)
        block_out = shot.astype(jnp.float32).reshape(H3 * W3, C3) + layer_scale * jnp.dot(hidden, w_reduce, preferred_element_type=jnp.float32)
        normed_two, inv_two = layer_norm(block_out)
        second = (normed_two * down_gain).astype(jnp.bfloat16)
        return (normed_one, inv_one, pre, normed_two, inv_two, second)

    def forward_shot(shot):
        second = forward_parts(shot)[5]
        patches = to_patches(second.reshape(H3, W3, C3))
        return jnp.dot(patches, w_down, preferred_element_type=jnp.float32).astype(jnp.bfloat16)

    def backward_shot(pair):
        shot, grad_tokens = pair
        normed_one, inv_one, pre, normed_two, inv_two, second = forward_parts(shot)
        group_width = C4 // N_SPACE
        left = grad_tokens.astype(jnp.float32).reshape(TILES, N_SPACE, group_width)
        right = w_down.astype(jnp.float32).reshape(4 * C3, N_SPACE, group_width)
        terms = jnp.einsum('tjc,pjc->jtp', left, right)
        terms = lax.optimization_barrier(terms.astype(jnp.bfloat16))
        grad_patches = lax.optimization_barrier(jnp.sum(terms.astype(jnp.float32), axis=0))
        grad_second = from_patches(grad_patches, H3, W3, C3).reshape(H3 * W3, C3)
        grad_block = norm_back(grad_second, normed_two, inv_two, down_gain)
        grad_scaled = (grad_block * layer_scale).astype(jnp.bfloat16)
        grad_hidden = jnp.dot(grad_scaled, w_reduce.T, preferred_element_type=jnp.float32)
        grad_pre = (grad_hidden * gelu_slope(pre)).astype(jnp.bfloat16)
        grad_first = jnp.dot(grad_pre, w_expand.T, preferred_element_type=jnp.float32)
        grad_mixed = norm_back(grad_first, normed_one, inv_one, mix_gain)
        return grad_mixed.astype(jnp.bfloat16).reshape(H3, W3, C3)
    tokens = lax.map(forward_shot, section_three)
    targets = owner_table[:, :, 0].astype(jnp.int32)
    ranks = jax.vmap(slot_ranks)(targets)
    slots = (jnp.arange(N_DP, dtype=jnp.int32)[:, None] * CAP + ranks).astype(jnp.int32)
    packed_tokens = jnp.zeros((N_DP, SLOTS, C4), jnp.bfloat16).at[targets.reshape(-1), slots.reshape(-1)].set(tokens.reshape(-1, C4))
    grad_tokens = grad_packed[targets, slots]
    grad_mixed = lax.map(backward_shot, (section_three, grad_tokens))
    return (packed_tokens, grad_mixed)
```

```python
import jax
import jax.numpy as jnp
from jax import lax
from jax.experimental import pallas as pl
from jax.experimental.pallas import tpu as pltpu
from jax.sharding import PartitionSpec as P

KS = 7
HALF = KS // 2
LANES = 128
LEFT = 8
F32 = jnp.float32
BF16 = jnp.bfloat16
VMEM = pl.BlockSpec(memory_space=pltpu.VMEM)
SMEM = pl.BlockSpec(memory_space=pltpu.SMEM)
ANY = pl.BlockSpec(memory_space=pl.ANY)


def call(body, ins, specs, outs, scratch, limit_mib, flops, moved, name):
    return pl.pallas_call(
        body,
        in_specs=specs,
        out_shape=tuple(jax.ShapeDtypeStruct(s, d) for s, d in outs),
        out_specs=tuple(VMEM for _ in outs),
        scratch_shapes=scratch,
        compiler_params=pltpu.CompilerParams(vmem_limit_bytes=limit_mib << 20),
        cost_estimate=pl.CostEstimate(
            flops=int(flops), bytes_accessed=int(moved), transcendentals=0
        ),
        name=name,
    )(*ins)


def nt(a, b):
    return lax.dot_general(a, b, (((1,), (1,)), ((), ())), preferred_element_type=F32)


def nn(a, b):
    return jnp.dot(a, b, preferred_element_type=F32)


def normalize(values):
    center = values - jnp.mean(values, axis=-1, keepdims=True)
    inv_std = lax.rsqrt(jnp.mean(center * center, axis=-1, keepdims=True) + 1e-06)
    return center * inv_std, inv_std


def norm_back(grad, normed, inv_std, gain):
    scaled = grad * gain
    return inv_std * (
        scaled
        - jnp.mean(scaled, axis=-1, keepdims=True)
        - normed * jnp.mean(scaled * normed, axis=-1, keepdims=True)
    )


def forward_body(
    rows, width, channels, hidden, block,
    place, x_ref, near_ref, far_ref, kernel_ref, bias_ref, gain_ref, w1_ref, w2_ref,
    scale_ref, down_gain_ref,
    patch_ref, slope_ref, n1_ref, inv1_ref, n2_ref, inv2_ref,
    padded, mixed, first, acc, grid,
):
    odd = place[0] % 2 == 1
    chunks = channels // LANES
    tall = rows + 2 * HALF
    padded[:, :, 0:LEFT, :] = jnp.zeros((chunks, tall, LEFT, LANES), F32)
    padded[:, :, LEFT + width :, :] = jnp.zeros((chunks, tall, LEFT, LANES), F32)

    def fill(c, _):
        at = pl.ds(pl.multiple_of(c * LANES, LANES), LANES)
        cols = pl.ds(LEFT, width)
        near, far = near_ref[0, :, :, at].astype(F32), far_ref[0, :, :, at].astype(F32)
        above, below = jnp.where(odd, near, far), jnp.where(odd, far, near)
        padded[c, 0:HALF, cols, :] = above[rows - HALF :]
        padded[c, HALF : HALF + rows, cols, :] = x_ref[0, :, :, at].astype(F32)
        padded[c, HALF + rows :, cols, :] = below[:HALF]
        total = [jnp.zeros((width, LANES), F32) for _ in range(rows)]
        for dx in range(KS):
            taps = [kernel_ref[dy, dx : dx + 1, at] for dy in range(KS)]
            for r in range(tall):
                line = padded[c, r, pl.ds(LEFT - HALF + dx, width), :]
                for out in range(rows):
                    if 0 <= r - out < KS:
                        total[out] = total[out] + line * taps[r - out]
        for out in range(rows):
            mixed[pl.ds(out * width, width), at] = total[out] + bias_ref[0:1, at]
        return 0

    lax.fori_loop(0, chunks, fill, 0)
    count = rows * width
    step = width
    for r in range(0, count, step):
        n1, inv1 = normalize(mixed[r : r + step, :])
        n1_ref[r : r + step, :] = n1
        inv1_ref[r : r + step, :] = jnp.broadcast_to(inv1, (step, LANES))
        first[r : r + step, :] = (n1 * gain_ref[...]).astype(BF16)
    for b in range(0, hidden, block):
        pre = nn(first[...], w1_ref[:, b : b + block])
        cumulative = 0.5 * (1.0 + lax.erf(pre * 0.7071067811865476))
        density = jnp.exp(-0.5 * pre * pre) * 0.3989422804014327
        slope_ref[:, b : b + block] = cumulative + pre * density
        term = nn((pre * cumulative).astype(BF16), w2_ref[b : b + block, :])
        if b == 0:
            acc[...] = term
        else:
            acc[...] += term
    for r in range(rows):
        at = pl.ds(r * width, width)
        v = x_ref[0, r].astype(F32) + scale_ref[...] * acc[at, :]
        n2, inv2 = normalize(v)
        n2_ref[at, :] = n2
        inv2_ref[at, :] = jnp.broadcast_to(inv2, (step, LANES))
        second = n2 * down_gain_ref[...]
        for c in range(chunks):
            grid[c, at, :] = second[:, c * LANES : (c + 1) * LANES]
    half = width // 2
    for r in range(rows // 2):
        for a in range(2):
            for b in range(2):
                piece = jnp.concatenate(
                    [
                        grid[c, pl.ds((2 * r + a) * width + b, half, stride=2), :]
                        for c in range(chunks)
                    ],
                    axis=1,
                )
                patch_ref[r * half : (r + 1) * half, (2 * a + b) * channels : (2 * a + b + 1) * channels] = (
                    piece.astype(BF16)
                )


def pull_body(
    spaces, owners, capacity,
    place, table_ref, returned_ref, w_ref, after_ref,
    keep_ref, send_ref, pick_ref,
    wanted, both,
):
    core = place[0] % 2
    targets = table_ref[0]
    count = targets.shape[0]
    wide = max(owners, LANES)
    hot = targets == lax.broadcasted_iota(jnp.int32, (count, wide), 1)
    hot_b = jnp.where(hot, 1.0, 0.0).astype(BF16)
    lower = lax.broadcasted_iota(jnp.int32, (count, count), 0) > lax.broadcasted_iota(
        jnp.int32, (count, count), 1
    )
    earlier = nn(jnp.where(lower, 1.0, 0.0).astype(BF16), hot_b)
    rank = jnp.sum(jnp.where(hot, earlier, 0.0), axis=1, keepdims=True).astype(jnp.int32)
    slots = returned_ref.shape[0]
    pick = jnp.where(
        targets * capacity + rank == lax.broadcasted_iota(jnp.int32, (count, slots), 1), 1.0, 0.0
    ).astype(BF16)
    pick_ref[...] = pick
    band = count // spaces
    wanted[...] = nn(pick, returned_ref[...]).astype(BF16).reshape(wanted.shape)
    chips = spaces // 2
    for i in range(chips):
        both[i * band : (i + 1) * band, :] = wanted[2 * i + core]
        both[(chips + i) * band : (chips + i + 1) * band, :] = wanted[2 * i + 1 - core]
    depth = w_ref.shape[0]
    step = 512
    for d in range(0, depth, step):
        part = nt(both[...], w_ref[d : d + step, :]).astype(BF16)
        for i in range(chips):
            keep_ref[i, :, d : d + step] = part[i * band : (i + 1) * band]
            send_ref[i, :, d : d + step] = part[(chips + i) * band : (chips + i + 1) * band]


def add_body(chips, place, keep_ref, near_ref, *outs):
    chip = place[0] // 2
    for j in range(1, chips):
        at = lax.rem(chip + j, chips)
        outs[j - 1][...] = (keep_ref[at].astype(F32) + near_ref[at].astype(F32)).astype(BF16)


def backward_body(
    rows, width, channels, hidden, block, chips,
    place, keep_ref, near_ref, *rest,
):
    far = rest[: chips - 1]
    (
        slope_ref, n1_ref, inv1_ref, n2_ref, inv2_ref, gain_ref, w1_ref, w2_ref, scale_ref,
        down_gain_ref, after_ref, out_ref, grid, scaled, acc,
    ) = rest[chips - 1 :]
    chip = place[0] // 2
    half = width // 2
    chunks = channels // LANES
    for r in range(rows // 2):
        for a in range(2):
            for b in range(2):
                at = (pl.ds(r * half, half), pl.ds((2 * a + b) * channels, channels))
                value = keep_ref[(chip,) + at].astype(F32) + near_ref[(chip,) + at].astype(F32)
                for piece in far:
                    value = value + piece[at].astype(F32)
                for c in range(chunks):
                    grid[c, pl.ds((2 * r + a) * width + b, half, stride=2), :] = (
                        value[:, c * LANES : (c + 1) * LANES]
                    )
    for r in range(rows):
        at = pl.ds(r * width, width)
        grad = jnp.concatenate([grid[c, at, :] for c in range(chunks)], axis=1)
        back = norm_back(grad, n2_ref[at, :], inv2_ref[at, 0:1], down_gain_ref[...])
        scaled[at, :] = (back * scale_ref[...]).astype(BF16)
    for b in range(0, hidden, block):
        grad_pre = (nt(scaled[...], w2_ref[b : b + block, :]) * slope_ref[:, b : b + block]).astype(BF16)
        term = nt(grad_pre, w1_ref[:, b : b + block])
        if b == 0:
            acc[...] = term
        else:
            acc[...] += term
    for r in range(rows):
        at = pl.ds(r * width, width)
        back = norm_back(acc[at, :], n1_ref[at, :], inv1_ref[at, 0:1], gain_ref[...])
        out_ref[0, r] = back.astype(BF16)


def push_body(chips, place, *rest):
    pieces = rest[: 2 * chips]
    pick_ref, w_ref, out_ref, patches, tokens = rest[2 * chips :]
    chip, core = place[0] // 2, place[0] % 2
    band = pieces[0].shape[0]
    for i, piece in enumerate(pieces):
        patches[i * band : (i + 1) * band, :] = piece[...]
    result = nn(patches[...], w_ref[...]).astype(BF16)
    for i in range(2 * chips):
        source = lax.rem(chip + chips - i // 2, chips)
        owner = 2 * source + (core if i % 2 == 0 else 1 - core)
        tokens[owner] = result[i * band : (i + 1) * band]
    flat = tokens[...].reshape(2 * chips * band, tokens.shape[2])
    out_ref[...] = lax.dot_general(
        pick_ref[...], flat, (((0,), (0,)), ((), ())), preferred_element_type=F32
    ).astype(BF16)


def on_device(
    section_three, dw_kernel, dw_bias, mix_gain, w_expand, w_reduce, layer_scale, down_gain,
    w_down, owner_table, grad_packed,
):
    owners = lax.axis_size("dp")
    spaces = lax.axis_size("space")
    chips = spaces // 2
    slots = grad_packed.shape[1]
    capacity = slots // owners
    _, rows, width, channels = section_three.shape
    hidden = w_expand.shape[1]
    count = rows * width
    band = count // 4
    tokens = owner_table.shape[1]
    deep, narrow = w_down.shape
    place = lax.axis_index("space").astype(jnp.int32).reshape(1)
    row = lambda v: v.reshape(1, -1)

    swap = [(i, i ^ 1) for i in range(spaces)]
    joints = [(i, i + 1) for i in range(1, spaces - 1, 2)]
    joints = joints + [(b, a) for a, b in joints]

    def onward(j):
        return [(i, (i + 2 * j) % spaces) for i in range(spaces)]

    near = lax.ppermute(section_three, "space", swap)
    far = lax.ppermute(section_three, "space", joints)
    returned = lax.all_to_all(grad_packed[0], "dp", split_axis=0, concat_axis=0, tiled=True)

    block = 256
    patches, slope, n1, inv1, n2, inv2 = call(
        lambda *refs: forward_body(rows, width, channels, hidden, block, *refs),
        (place, section_three, near, far, dw_kernel, row(dw_bias), row(mix_gain), w_expand, w_reduce,
         row(layer_scale), row(down_gain)),
        [SMEM] + [VMEM] * 10,
        [((band, 4 * channels), BF16), ((count, hidden), F32), ((count, channels), F32),
         ((count, LANES), F32), ((count, channels), F32), ((count, LANES), F32)],
        [pltpu.VMEM((channels // LANES, rows + 2 * HALF, width + 2 * LEFT, LANES), F32),
         pltpu.VMEM((count, channels), F32), pltpu.VMEM((count, channels), BF16),
         pltpu.VMEM((count, channels), F32), pltpu.VMEM((channels // LANES, count, LANES), F32)],
        24, 4 * count * channels * hidden, 9e6, "forward",
    )
    held = [patches] + [lax.ppermute(patches, "space", onward(j)) for j in range(1, chips)]
    keep, send, pick = call(
        lambda *refs: pull_body(spaces, owners, capacity, *refs),
        (place, owner_table, returned, w_down, inv2),
        [SMEM, VMEM, VMEM, VMEM, ANY],
        [((chips, band, deep), BF16), ((chips, band, deep), BF16), ((tokens, slots), BF16)],
        [pltpu.VMEM((spaces, band, narrow), BF16), pltpu.VMEM((tokens, narrow), BF16)],
        16, 2 * tokens * deep * narrow, 4e6, "pull",
    )
    sent = lax.ppermute(send, "space", swap)
    sums = call(
        lambda *refs: add_body(chips, *refs),
        (place, keep, sent), [SMEM, VMEM, VMEM],
        [((band, deep), BF16)] * (chips - 1), [], 8, 2e6, 1e6, "add",
    )
    across = [lax.ppermute(sums[j - 1], "space", onward(j)) for j in range(1, chips)]
    pieces = []
    for piece in held:
        pieces += [piece, lax.ppermute(piece, "space", swap)]
    (buffer,) = call(
        lambda *refs: push_body(chips, *refs),
        (place, *pieces, pick, w_down),
        [SMEM] + [VMEM] * (len(pieces) + 2),
        [((slots, narrow), BF16)],
        [pltpu.VMEM((tokens, deep), BF16), pltpu.VMEM((spaces, band, narrow), BF16)],
        16, 2 * tokens * deep * narrow, 4e6, "push",
    )
    arrived = lax.all_to_all(buffer, "dp", split_axis=0, concat_axis=0, tiled=True)
    (grad_mixed,) = call(
        lambda *refs: backward_body(rows, width, channels, hidden, block, chips, *refs),
        (place, keep, sent, *across, slope, n1, inv1, n2, inv2, row(mix_gain), w_expand, w_reduce,
         row(layer_scale), row(down_gain), buffer),
        [SMEM] + [VMEM] * (11 + chips) + [ANY],
        [(section_three.shape, BF16)],
        [pltpu.VMEM((channels // LANES, count, LANES), F32), pltpu.VMEM((count, channels), BF16),
         pltpu.VMEM((count, channels), F32)],
        24, 4 * count * channels * hidden, 9e6, "backward",
    )
    return arrived[None], grad_mixed


def solution(mesh):
    in_specs = (
        P("dp", "space", None, None), P(), P(), P(), P(), P(), P(), P(), P(None, "space"),
        P("dp", None, None), P("dp", None, "space"),
    )
    out_specs = (P("dp", None, "space"), P("dp", "space", None, None))
    return jax.shard_map(
        on_device, mesh=mesh, in_specs=in_specs, out_specs=out_specs, check_vma=False
    )
```

```python
import jax
import jax.numpy as jnp
from jax import lax
from jax.experimental import pallas as pl
from jax.experimental.pallas import tpu as pltpu
from jax.sharding import PartitionSpec as P


KS = 7
HALF = KS // 2
LANES = 128
LEFT = 8
F32 = jnp.float32
BF16 = jnp.bfloat16
VMEM = pl.BlockSpec(memory_space=pltpu.VMEM)
SMEM = pl.BlockSpec(memory_space=pltpu.SMEM)
HBM = pl.BlockSpec(memory_space=pltpu.HBM)


def call(body, ins, specs, outs, scratch, limit_mib, flops, moved):
    return pl.pallas_call(
        body,
        in_specs=specs,
        out_shape=tuple(jax.ShapeDtypeStruct(s, d) for s, d in outs),
        out_specs=tuple(VMEM for _ in outs),
        scratch_shapes=scratch,
        compiler_params=pltpu.CompilerParams(vmem_limit_bytes=limit_mib << 20),
        cost_estimate=pl.CostEstimate(
            flops=int(flops), bytes_accessed=int(moved), transcendentals=0
        ),
    )(*ins)


def nt(a, b):
    return lax.dot_general(a, b, (((1,), (1,)), ((), ())), preferred_element_type=F32)


def nn(a, b):
    return jnp.dot(a, b, preferred_element_type=F32)


def normalize(values):
    center = values - jnp.mean(values, axis=-1, keepdims=True)
    inv_std = lax.rsqrt(jnp.mean(center * center, axis=-1, keepdims=True) + 1e-06)
    return center * inv_std, inv_std


def norm_back(grad, normed, inv_std, gain):
    scaled = grad * gain
    return inv_std * (
        scaled
        - jnp.mean(scaled, axis=-1, keepdims=True)
        - normed * jnp.mean(scaled * normed, axis=-1, keepdims=True)
    )


def fetch(hidden, block, w1_hbm, w1_ref, w2_hbm, w2_ref, sems):
    loads = []
    for i, b in enumerate(range(0, hidden, block)):
        cols, lines = (slice(None), pl.ds(b, block)), pl.ds(b, block)
        loads.append(
            (
                pltpu.make_async_copy(w1_hbm.at[cols], w1_ref.at[cols], sems.at[0, i]),
                pltpu.make_async_copy(w2_hbm.at[lines], w2_ref.at[lines], sems.at[1, i]),
            )
        )
        loads[-1][0].start()
        loads[-1][1].start()
    return loads


def forward_body(
    rows, width, channels, hidden, block,
    place, x_ref, near_ref, far_ref, kernel_ref, bias_ref, gain_ref, w1_hbm, w2_hbm,
    scale_ref, down_gain_ref,
    patch_ref, slope_ref, n1_ref, inv1_ref, n2_ref, inv2_ref,
    padded, mixed, first, acc, grid, w1_ref, w2_ref, sems,
):
    loads = fetch(hidden, block, w1_hbm, w1_ref, w2_hbm, w2_ref, sems)
    odd = place[0] % 2 == 1
    chunks = channels // LANES
    tall = rows + 2 * HALF
    padded[:, :, 0:LEFT, :] = jnp.zeros((chunks, tall, LEFT, LANES), F32)
    padded[:, :, LEFT + width :, :] = jnp.zeros((chunks, tall, LEFT, LANES), F32)

    def fill(c, _):
        at = pl.ds(pl.multiple_of(c * LANES, LANES), LANES)
        cols = pl.ds(LEFT, width)
        near, far = near_ref[0, :, :, at].astype(F32), far_ref[0, :, :, at].astype(F32)
        above, below = jnp.where(odd, near, far), jnp.where(odd, far, near)
        padded[c, 0:HALF, cols, :] = above[rows - HALF :]
        padded[c, HALF : HALF + rows, cols, :] = x_ref[0, :, :, at].astype(F32)
        padded[c, HALF + rows :, cols, :] = below[:HALF]
        total = [jnp.zeros((width, LANES), F32) for _ in range(rows)]
        for dx in range(KS):
            taps = [kernel_ref[dy, dx : dx + 1, at] for dy in range(KS)]
            for r in range(tall):
                line = padded[c, r, pl.ds(LEFT - HALF + dx, width), :]
                for out in range(rows):
                    if 0 <= r - out < KS:
                        total[out] = total[out] + line * taps[r - out]
        for out in range(rows):
            mixed[pl.ds(out * width, width), at] = total[out] + bias_ref[at].reshape(1, LANES)
        return 0

    lax.fori_loop(0, chunks, fill, 0)
    count = rows * width
    step = width
    for r in range(0, count, step):
        n1, inv1 = normalize(mixed[r : r + step, :])
        n1_ref[r : r + step, :] = n1
        inv1_ref[r : r + step, :] = jnp.broadcast_to(inv1, (step, LANES))
        first[r : r + step, :] = (n1 * gain_ref[...].reshape(1, channels)).astype(BF16)
    for i, b in enumerate(range(0, hidden, block)):
        loads[i][0].wait()
        loads[i][1].wait()
        pre = nn(first[...], w1_ref[:, b : b + block])
        cumulative = 0.5 * (1.0 + lax.erf(pre * 0.7071067811865476))
        density = jnp.exp(-0.5 * pre * pre) * 0.3989422804014327
        slope_ref[:, b : b + block] = cumulative + pre * density
        term = nn((pre * cumulative).astype(BF16), w2_ref[b : b + block, :])
        if b == 0:
            acc[...] = term
        else:
            acc[...] += term
    for r in range(rows):
        at = pl.ds(r * width, width)
        v = x_ref[0, r].astype(F32) + scale_ref[...].reshape(1, channels) * acc[at, :]
        n2, inv2 = normalize(v)
        n2_ref[at, :] = n2
        inv2_ref[at, :] = jnp.broadcast_to(inv2, (step, LANES))
        second = n2 * down_gain_ref[...].reshape(1, channels)
        for c in range(chunks):
            grid[c, at, :] = second[:, c * LANES : (c + 1) * LANES]
    half = width // 2
    for r in range(rows // 2):
        for a in range(2):
            for b in range(2):
                piece = jnp.concatenate(
                    [
                        grid[c, pl.ds((2 * r + a) * width + b, half, stride=2), :]
                        for c in range(chunks)
                    ],
                    axis=1,
                )
                patch_ref[r * half : (r + 1) * half, (2 * a + b) * channels : (2 * a + b + 1) * channels] = (
                    piece.astype(BF16)
                )


def pull_body(
    spaces, owners, capacity, step,
    place, table_ref, returned_ref, w_hbm,
    keep_ref, send_ref, pick_ref,
    wanted, both, w_ref, sems,
):
    depth = w_ref.shape[0]
    loads = []
    for i, d in enumerate(range(0, depth, step)):
        lines = pl.ds(d, step)
        loads.append(pltpu.make_async_copy(w_hbm.at[lines], w_ref.at[lines], sems.at[i]))
        loads[-1].start()
    core = place[0] % 2
    targets = table_ref[...]
    count = targets.shape[1]
    tall = max(owners, 16)
    hot = targets == lax.broadcasted_iota(jnp.int32, (tall, count), 0)
    sooner = lax.broadcasted_iota(jnp.int32, (count, count), 0) < lax.broadcasted_iota(
        jnp.int32, (count, count), 1
    )
    earlier = nn(jnp.where(hot, 1.0, 0.0).astype(BF16), jnp.where(sooner, 1.0, 0.0).astype(BF16))
    rank = jnp.sum(jnp.where(hot, earlier, 0.0), axis=0, keepdims=True).astype(jnp.int32)
    slots = returned_ref.shape[0]
    pick = jnp.where(
        targets * capacity + rank == lax.broadcasted_iota(jnp.int32, (slots, count), 0), 1.0, 0.0
    ).astype(BF16)
    pick_ref[...] = pick
    band = count // spaces
    wanted[...] = (
        lax.dot_general(pick, returned_ref[...], (((0,), (0,)), ((), ())), preferred_element_type=F32)
        .astype(BF16)
        .reshape(wanted.shape)
    )
    chips = spaces // 2
    for i in range(chips):
        both[i * band : (i + 1) * band, :] = wanted[2 * i + core]
        both[(chips + i) * band : (chips + i + 1) * band, :] = wanted[2 * i + 1 - core]
    for n, d in enumerate(range(0, depth, step)):
        loads[n].wait()
        part = nt(both[...], w_ref[d : d + step, :]).astype(BF16)
        for i in range(chips):
            keep_ref[i, :, d : d + step] = part[i * band : (i + 1) * band]
            send_ref[i, :, d : d + step] = part[(chips + i) * band : (chips + i + 1) * band]


def add_body(chips, place, keep_ref, near_ref, *outs):
    chip = place[0] // 2
    for j in range(1, chips):
        at = lax.rem(chip + j, chips)
        outs[j - 1][...] = (keep_ref[at].astype(F32) + near_ref[at].astype(F32)).astype(BF16)


def backward_body(
    rows, width, channels, hidden, block, chips,
    place, keep_ref, near_ref, *rest,
):
    far = rest[: chips - 1]
    (
        slope_ref, n1_ref, inv1_ref, n2_ref, inv2_ref, gain_ref, w1_hbm, w2_hbm, scale_ref,
        down_gain_ref, out_ref, grid, scaled, acc, w1_ref, w2_ref, sems,
    ) = rest[chips - 1 :]
    loads = fetch(hidden, block, w1_hbm, w1_ref, w2_hbm, w2_ref, sems)
    chip = place[0] // 2
    half = width // 2
    chunks = channels // LANES
    for r in range(rows // 2):
        for a in range(2):
            for b in range(2):
                at = (pl.ds(r * half, half), pl.ds((2 * a + b) * channels, channels))
                value = keep_ref[(chip,) + at].astype(F32) + near_ref[(chip,) + at].astype(F32)
                for piece in far:
                    value = value + piece[at].astype(F32)
                for c in range(chunks):
                    grid[c, pl.ds((2 * r + a) * width + b, half, stride=2), :] = (
                        value[:, c * LANES : (c + 1) * LANES]
                    )
    for r in range(rows):
        at = pl.ds(r * width, width)
        grad = jnp.concatenate([grid[c, at, :] for c in range(chunks)], axis=1)
        back = norm_back(grad, n2_ref[at, :], inv2_ref[at, 0:1], down_gain_ref[...].reshape(1, channels))
        scaled[at, :] = (back * scale_ref[...].reshape(1, channels)).astype(BF16)
    for i, b in enumerate(range(0, hidden, block)):
        loads[i][0].wait()
        loads[i][1].wait()
        grad_pre = (nt(scaled[...], w2_ref[b : b + block, :]) * slope_ref[:, b : b + block]).astype(BF16)
        term = nt(grad_pre, w1_ref[:, b : b + block])
        if b == 0:
            acc[...] = term
        else:
            acc[...] += term
    for r in range(rows):
        at = pl.ds(r * width, width)
        back = norm_back(acc[at, :], n1_ref[at, :], inv1_ref[at, 0:1], gain_ref[...].reshape(1, channels))
        out_ref[0, r] = back.astype(BF16)


def push_body(chips, step, place, *rest):
    pieces = rest[: 2 * chips]
    pick_ref, w_hbm, out_ref, patches, tokens, w_ref, sems = rest[2 * chips :]
    loads = []
    depth = w_ref.shape[0]
    for i, d in enumerate(range(0, depth, step)):
        lines = pl.ds(d, step)
        loads.append(pltpu.make_async_copy(w_hbm.at[lines], w_ref.at[lines], sems.at[i]))
        loads[-1].start()
    chip, core = place[0] // 2, place[0] % 2
    band = pieces[0].shape[0]
    for i, piece in enumerate(pieces):
        patches[i * band : (i + 1) * band, :] = piece[...]
    result = 0.0
    for i, d in enumerate(range(0, depth, step)):
        loads[i].wait()
        result = result + nn(patches[:, d : d + step], w_ref[d : d + step, :])
    result = result.astype(BF16)
    for i in range(2 * chips):
        source = lax.rem(chip + chips - i // 2, chips)
        owner = 2 * source + (core if i % 2 == 0 else 1 - core)
        tokens[owner] = result[i * band : (i + 1) * band]
    flat = tokens[...].reshape(2 * chips * band, tokens.shape[2])
    out_ref[...] = nn(pick_ref[...], flat).astype(BF16)


def on_device(
    section_three, dw_kernel, dw_bias, mix_gain, w_expand, w_reduce, layer_scale, down_gain,
    w_down, owner_table, grad_packed,
):
    owners = lax.axis_size("dp")
    spaces = lax.axis_size("space")
    chips = spaces // 2
    slots = grad_packed.shape[1]
    capacity = slots // owners
    _, rows, width, channels = section_three.shape
    hidden = w_expand.shape[1]
    count = rows * width
    band = count // 4
    tokens = owner_table.shape[1]
    deep, narrow = w_down.shape
    place = lax.axis_index("space").astype(jnp.int32).reshape(1)
    block, step = 256, 768
    weights = [
        pltpu.VMEM(w_expand.shape, BF16), pltpu.VMEM(w_reduce.shape, BF16),
        pltpu.SemaphoreType.DMA((2, hidden // block)),
    ]
    down = [pltpu.VMEM(w_down.shape, BF16), pltpu.SemaphoreType.DMA((deep // step,))]

    swap = [(i, i ^ 1) for i in range(spaces)]
    joints = [(i, i + 1) for i in range(1, spaces - 1, 2)]
    joints = joints + [(b, a) for a, b in joints]

    def send(value, pairs):
        return lax.ppermute(value, "space", pairs)

    def trade(value):
        return lax.all_to_all(value, "dp", split_axis=0, concat_axis=0, tiled=True)

    def onward(j):
        return [(i, (i + 2 * j) % spaces) for i in range(spaces)]

    near = send(section_three, swap)
    far = send(section_three, joints)
    returned = trade(grad_packed[0])

    patches, slope, n1, inv1, n2, inv2 = call(
        lambda *refs: forward_body(rows, width, channels, hidden, block, *refs),
        (place, section_three, near, far, dw_kernel, dw_bias, mix_gain, w_expand, w_reduce,
         layer_scale, down_gain),
        [SMEM] + [VMEM] * 6 + [HBM] * 2 + [VMEM] * 2,
        [((band, 4 * channels), BF16), ((count, hidden), F32), ((count, channels), F32),
         ((count, LANES), F32), ((count, channels), F32), ((count, LANES), F32)],
        [pltpu.VMEM((channels // LANES, rows + 2 * HALF, width + 2 * LEFT, LANES), F32),
         pltpu.VMEM((count, channels), F32), pltpu.VMEM((count, channels), BF16),
         pltpu.VMEM((count, channels), F32), pltpu.VMEM((channels // LANES, count, LANES), F32)] + weights,
        20, 4 * count * channels * hidden, 9e6,
    )
    held = [patches] + [send(patches, onward(j)) for j in range(1, chips)]
    keep, give, pick = call(
        lambda *refs: pull_body(spaces, owners, capacity, step, *refs),
        (place, owner_table.reshape(1, tokens), returned, w_down),
        [SMEM, VMEM, VMEM, HBM],
        [((chips, band, deep), BF16), ((chips, band, deep), BF16), ((slots, tokens), BF16)],
        [pltpu.VMEM((spaces, band, narrow), BF16), pltpu.VMEM((tokens, narrow), BF16)] + down,
        12, 2 * tokens * deep * narrow, 4e6,
    )
    sent = send(give, swap)
    sums = call(
        lambda *refs: add_body(chips, *refs),
        (place, keep, sent), [SMEM, VMEM, VMEM],
        [((band, deep), BF16)] * (chips - 1), [], 4, 2e6, 1e6,
    )
    across = [send(sums[j - 1], onward(j)) for j in range(1, chips)]
    pieces = []
    for piece in held:
        pieces += [piece, send(piece, swap)]
    (buffer,) = call(
        lambda *refs: push_body(chips, step, *refs),
        (place, *pieces, pick, w_down),
        [SMEM] + [VMEM] * (len(pieces) + 1) + [HBM],
        [((slots, narrow), BF16)],
        [pltpu.VMEM((tokens, deep), BF16), pltpu.VMEM((spaces, band, narrow), BF16)] + down,
        12, 2 * tokens * deep * narrow, 4e6,
    )
    arrived = trade(buffer)
    (grad_mixed,) = call(
        lambda *refs: backward_body(rows, width, channels, hidden, block, chips, *refs),
        (place, keep, sent, *across, slope, n1, inv1, n2, inv2, mix_gain, w_expand, w_reduce,
         layer_scale, down_gain),
        [SMEM] + [VMEM] * (7 + chips) + [HBM] * 2 + [VMEM] * 2,
        [(section_three.shape, BF16)],
        [pltpu.VMEM((channels // LANES, count, LANES), F32), pltpu.VMEM((count, channels), BF16),
         pltpu.VMEM((count, channels), F32)] + weights,
        16, 4 * count * channels * hidden, 9e6,
    )
    return arrived[None], grad_mixed


def solution(mesh):
    in_specs = (
        P("dp", "space", None, None), P(), P(), P(), P(), P(), P(), P(), P(None, "space"),
        P("dp", None, None), P("dp", None, "space"),
    )
    out_specs = (P("dp", None, "space"), P("dp", "space", None, None))
    return jax.shard_map(
        on_device, mesh=mesh, in_specs=in_specs, out_specs=out_specs, check_vma=False
    )
```

```python
import jax
import jax.numpy as jnp
from jax import lax
from jax.experimental import pallas as pl
from jax.experimental.pallas import tpu as pltpu
from jax.sharding import PartitionSpec as P


KS = 7
HALF = KS // 2
LANES = 128
LEFT = 8
F32 = jnp.float32
BF16 = jnp.bfloat16
VMEM = pl.BlockSpec(memory_space=pltpu.VMEM)
SMEM = pl.BlockSpec(memory_space=pltpu.SMEM)
HBM = pl.BlockSpec(memory_space=pltpu.HBM)


def far_off(*values):
    return tuple(pltpu.with_memory_space_constraint(v, pltpu.HBM) for v in values)


def close(*values):
    return tuple(pltpu.with_memory_space_constraint(v, pltpu.VMEM) for v in values)


def start(copies):
    for copy in copies:
        copy.start()


def wait(copies):
    for copy in copies:
        copy.wait()


def call(body, ins, specs, outs, scratch, limit_mib, flops, moved):
    return pl.pallas_call(
        body,
        in_specs=specs,
        out_shape=tuple(o if isinstance(o, jax.ShapeDtypeStruct) else pltpu.VMEM(*o) for o in outs),
        out_specs=tuple(HBM if isinstance(o, jax.ShapeDtypeStruct) else VMEM for o in outs),
        scratch_shapes=scratch,
        compiler_params=pltpu.CompilerParams(vmem_limit_bytes=limit_mib << 20),
        cost_estimate=pl.CostEstimate(
            flops=int(flops), bytes_accessed=int(moved), transcendentals=0
        ),
    )(*ins)


def nt(a, b):
    return lax.dot_general(a, b, (((1,), (1,)), ((), ())), preferred_element_type=F32)


def nn(a, b):
    return jnp.dot(a, b, preferred_element_type=F32)


def normalize(values):
    center = values - jnp.mean(values, axis=-1, keepdims=True)
    inv_std = lax.rsqrt(jnp.mean(center * center, axis=-1, keepdims=True) + 1e-06)
    return center * inv_std, inv_std


def norm_back(grad, normed, inv_std, gain):
    scaled = grad * gain
    return inv_std * (
        scaled
        - jnp.mean(scaled, axis=-1, keepdims=True)
        - normed * jnp.mean(scaled * normed, axis=-1, keepdims=True)
    )


def fetch(hidden, block, w1_hbm, w1_ref, w2_hbm, w2_ref, sems):
    loads = []
    for i, b in enumerate(range(0, hidden, block)):
        cols, lines = (slice(None), pl.ds(b, block)), pl.ds(b, block)
        loads.append(
            (
                pltpu.make_async_copy(w1_hbm.at[cols], w1_ref.at[cols], sems.at[0, i]),
                pltpu.make_async_copy(w2_hbm.at[lines], w2_ref.at[lines], sems.at[1, i]),
            )
        )
        loads[-1][0].start()
        loads[-1][1].start()
    return loads


def forward_body(
    rows, width, channels, hidden, block,
    place, near_ref, far_ref, x_hbm, kernel_hbm, bias_hbm, gain_hbm, w1_hbm, w2_hbm,
    scale_hbm, down_gain_hbm,
    patch_ref, slope_ref, n1_ref, inv1_ref, n2_ref, inv2_ref,
    x_ref, kernel_ref, bias_ref, gain_ref, scale_ref, down_gain_ref,
    padded, mixed, first, acc, grid, small_sems, band_sems, w1_ref, w2_ref, sems,
):
    odd = place[0] % 2 == 1
    chunks = channels // LANES
    tall = rows + 2 * HALF
    sources = (kernel_hbm, bias_hbm, gain_hbm, scale_hbm, down_gain_hbm)
    targets = (kernel_ref, bias_ref, gain_ref, scale_ref, down_gain_ref)
    small = [pltpu.make_async_copy(s, t, small_sems.at[i]) for i, (s, t) in enumerate(zip(sources, targets))]

    def bands(c):
        at = (0, slice(None), slice(None), pl.ds(pl.multiple_of(c * LANES, LANES), LANES))
        return [pltpu.make_async_copy(x_hbm.at[at], x_ref.at[c], band_sems.at[c])]

    start(small[:2])
    for c in range(chunks):
        start(bands(c))
    start(small[2:])
    loads = fetch(hidden, block, w1_hbm, w1_ref, w2_hbm, w2_ref, sems)
    padded[:, :, 0:LEFT, :] = jnp.zeros((chunks, tall, LEFT, LANES), F32)
    padded[:, :, LEFT + width :, :] = jnp.zeros((chunks, tall, LEFT, LANES), F32)
    wait(small[:2])

    def fill(c, _):
        at = pl.ds(pl.multiple_of(c * LANES, LANES), LANES)
        cols = pl.ds(LEFT, width)
        wait(bands(c))
        near, far = near_ref[0, :, :, at].astype(F32), far_ref[0, :, :, at].astype(F32)
        above, below = jnp.where(odd, near, far), jnp.where(odd, far, near)
        padded[c, 0:HALF, cols, :] = above[rows - HALF :]
        padded[c, HALF : HALF + rows, cols, :] = x_ref[c].astype(F32)
        padded[c, HALF + rows :, cols, :] = below[:HALF]
        total = [jnp.zeros((width, LANES), F32) for _ in range(rows)]
        for dx in range(KS):
            taps = [kernel_ref[dy, dx : dx + 1, at] for dy in range(KS)]
            for r in range(tall):
                line = padded[c, r, pl.ds(LEFT - HALF + dx, width), :]
                for out in range(rows):
                    if 0 <= r - out < KS:
                        total[out] = total[out] + line * taps[r - out]
        for out in range(rows):
            mixed[pl.ds(out * width, width), at] = total[out] + bias_ref[at].reshape(1, LANES)
        return 0

    lax.fori_loop(0, chunks, fill, 0)
    wait(small[2:])
    count = rows * width
    step = width
    for r in range(0, count, step):
        n1, inv1 = normalize(mixed[r : r + step, :])
        n1_ref[r : r + step, :] = n1
        inv1_ref[r : r + step, :] = jnp.broadcast_to(inv1, (step, LANES))
        first[r : r + step, :] = (n1 * gain_ref[...].reshape(1, channels)).astype(BF16)
    for i, b in enumerate(range(0, hidden, block)):
        loads[i][0].wait()
        loads[i][1].wait()
        pre = nn(first[...], w1_ref[:, b : b + block])
        cumulative = 0.5 * (1.0 + lax.erf(pre * 0.7071067811865476))
        density = jnp.exp(-0.5 * pre * pre) * 0.3989422804014327
        slope_ref[:, b : b + block] = cumulative + pre * density
        term = nn((pre * cumulative).astype(BF16), w2_ref[b : b + block, :])
        if b == 0:
            acc[...] = term
        else:
            acc[...] += term
    for r in range(rows):
        at = pl.ds(r * width, width)
        line = jnp.concatenate([x_ref[c, r] for c in range(chunks)], axis=1)
        v = line.astype(F32) + scale_ref[...].reshape(1, channels) * acc[at, :]
        n2, inv2 = normalize(v)
        n2_ref[at, :] = n2
        inv2_ref[at, :] = jnp.broadcast_to(inv2, (step, LANES))
        second = n2 * down_gain_ref[...].reshape(1, channels)
        for c in range(chunks):
            grid[c, at, :] = second[:, c * LANES : (c + 1) * LANES]
    half = width // 2
    for r in range(rows // 2):
        for a in range(2):
            for b in range(2):
                piece = jnp.concatenate(
                    [
                        grid[c, pl.ds((2 * r + a) * width + b, half, stride=2), :]
                        for c in range(chunks)
                    ],
                    axis=1,
                )
                patch_ref[r * half : (r + 1) * half, (2 * a + b) * channels : (2 * a + b + 1) * channels] = (
                    piece.astype(BF16)
                )


def pull_body(
    spaces, owners, capacity, step,
    place, returned_ref, table_hbm, w_hbm,
    keep_ref, send_ref, pick_ref, w_ref,
    table_ref, wanted, both, small_sems, sems,
):
    depth = w_ref.shape[0]
    small = [pltpu.make_async_copy(table_hbm, table_ref, small_sems.at[0])]
    start(small)
    loads = []
    for i, d in enumerate(range(0, depth, step)):
        lines = pl.ds(d, step)
        loads.append(pltpu.make_async_copy(w_hbm.at[lines], w_ref.at[lines], sems.at[i]))
        loads[-1].start()
    core = place[0] % 2
    small[0].wait()
    targets = table_ref[...]
    count = targets.shape[1]
    tall = max(owners, 16)
    hot = targets == lax.broadcasted_iota(jnp.int32, (tall, count), 0)
    sooner = lax.broadcasted_iota(jnp.int32, (count, count), 0) < lax.broadcasted_iota(
        jnp.int32, (count, count), 1
    )
    earlier = nn(jnp.where(hot, 1.0, 0.0).astype(BF16), jnp.where(sooner, 1.0, 0.0).astype(BF16))
    rank = jnp.sum(jnp.where(hot, earlier, 0.0), axis=0, keepdims=True).astype(jnp.int32)
    slots = returned_ref.shape[0]
    pick = jnp.where(
        targets * capacity + rank == lax.broadcasted_iota(jnp.int32, (slots, count), 0), 1.0, 0.0
    ).astype(BF16)
    pick_ref[...] = pick
    band = count // spaces
    wanted[...] = (
        lax.dot_general(pick, returned_ref[...], (((0,), (0,)), ((), ())), preferred_element_type=F32)
        .astype(BF16)
        .reshape(wanted.shape)
    )
    chips = spaces // 2
    for i in range(chips):
        both[i * band : (i + 1) * band, :] = wanted[2 * i + core]
        both[(chips + i) * band : (chips + i + 1) * band, :] = wanted[2 * i + 1 - core]
    for n, d in enumerate(range(0, depth, step)):
        loads[n].wait()
        part = nt(both[...], w_ref[d : d + step, :]).astype(BF16)
        for i in range(chips):
            keep_ref[i, :, d : d + step] = part[i * band : (i + 1) * band]
            send_ref[i, :, d : d + step] = part[(chips + i) * band : (chips + i + 1) * band]


def add_body(chips, place, keep_ref, near_ref, *outs):
    chip = place[0] // 2
    for j in range(1, chips):
        at = lax.rem(chip + j, chips)
        outs[j - 1][...] = (keep_ref[at].astype(F32) + near_ref[at].astype(F32)).astype(BF16)


def backward_body(
    rows, width, channels, hidden, block, chips,
    place, keep_ref, near_ref, *rest,
):
    far = rest[: chips - 1]
    (
        slope_ref, n1_ref, inv1_ref, n2_ref, inv2_ref, gain_hbm, w1_hbm, w2_hbm, scale_hbm,
        down_gain_hbm, out_hbm, gain_ref, scale_ref, down_gain_ref, out_ref, grid, scaled, acc,
        small_sems, out_sems, w1_ref, w2_ref, sems,
    ) = rest[chips - 1 :]
    sources, targets = (down_gain_hbm, scale_hbm, gain_hbm), (down_gain_ref, scale_ref, gain_ref)
    small = [pltpu.make_async_copy(s, t, small_sems.at[i]) for i, (s, t) in enumerate(zip(sources, targets))]
    start(small)
    loads = fetch(hidden, block, w1_hbm, w1_ref, w2_hbm, w2_ref, sems)
    chip = place[0] // 2
    half = width // 2
    chunks = channels // LANES
    for r in range(rows // 2):
        for a in range(2):
            for b in range(2):
                at = (pl.ds(r * half, half), pl.ds((2 * a + b) * channels, channels))
                value = keep_ref[(chip,) + at].astype(F32) + near_ref[(chip,) + at].astype(F32)
                for piece in far:
                    value = value + piece[at].astype(F32)
                for c in range(chunks):
                    grid[c, pl.ds((2 * r + a) * width + b, half, stride=2), :] = (
                        value[:, c * LANES : (c + 1) * LANES]
                    )
    wait(small)
    for r in range(rows):
        at = pl.ds(r * width, width)
        grad = jnp.concatenate([grid[c, at, :] for c in range(chunks)], axis=1)
        back = norm_back(grad, n2_ref[at, :], inv2_ref[at, 0:1], down_gain_ref[...].reshape(1, channels))
        scaled[at, :] = (back * scale_ref[...].reshape(1, channels)).astype(BF16)
    for i, b in enumerate(range(0, hidden, block)):
        loads[i][0].wait()
        loads[i][1].wait()
        grad_pre = (nt(scaled[...], w2_ref[b : b + block, :]) * slope_ref[:, b : b + block]).astype(BF16)
        term = nt(grad_pre, w1_ref[:, b : b + block])
        if b == 0:
            acc[...] = term
        else:
            acc[...] += term
    stores = []
    for r in range(rows):
        at = pl.ds(r * width, width)
        back = norm_back(acc[at, :], n1_ref[at, :], inv1_ref[at, 0:1], gain_ref[...].reshape(1, channels))
        out_ref[0, r] = back.astype(BF16)
        stores.append(pltpu.make_async_copy(out_ref.at[0, r], out_hbm.at[0, r], out_sems.at[r]))
        stores[-1].start()
    wait(stores)


def push_body(chips, place, *rest):
    pieces = rest[: 2 * chips]
    pick_ref, w_ref, out_ref, patches, tokens = rest[2 * chips :]
    chip, core = place[0] // 2, place[0] % 2
    band = pieces[0].shape[0]
    for i, piece in enumerate(pieces):
        patches[i * band : (i + 1) * band, :] = piece[...]
    result = nn(patches[...], w_ref[...]).astype(BF16)
    for i in range(2 * chips):
        source = lax.rem(chip + chips - i // 2, chips)
        owner = 2 * source + (core if i % 2 == 0 else 1 - core)
        tokens[owner] = result[i * band : (i + 1) * band]
    flat = tokens[...].reshape(2 * chips * band, tokens.shape[2])
    out_ref[...] = nn(pick_ref[...], flat).astype(BF16)


def on_device(
    section_three, dw_kernel, dw_bias, mix_gain, w_expand, w_reduce, layer_scale, down_gain,
    w_down, owner_table, grad_packed,
):
    owners = lax.axis_size("dp")
    spaces = lax.axis_size("space")
    chips = spaces // 2
    slots = grad_packed.shape[1]
    capacity = slots // owners
    _, rows, width, channels = section_three.shape
    hidden = w_expand.shape[1]
    count = rows * width
    band = count // 4
    tokens = owner_table.shape[1]
    deep, narrow = w_down.shape
    place = lax.axis_index("space").astype(jnp.int32).reshape(1)
    block, step = 256, 768
    weights = [
        pltpu.VMEM(w_expand.shape, BF16), pltpu.VMEM(w_reduce.shape, BF16),
        pltpu.SemaphoreType.DMA((2, hidden // block)),
    ]

    swap = [(i, i ^ 1) for i in range(spaces)]
    joints = [(i, i + 1) for i in range(1, spaces - 1, 2)]
    joints = joints + [(b, a) for a, b in joints]

    def send(value, pairs):
        return lax.ppermute(value, "space", pairs)

    def trade(value):
        return lax.all_to_all(value, "dp", split_axis=0, concat_axis=0, tiled=True)

    def onward(j):
        return [(i, (i + 2 * j) % spaces) for i in range(spaces)]

    near = send(section_three, swap)
    far = send(section_three, joints)
    returned = trade(grad_packed[0])

    vector = pltpu.VMEM((channels,), F32)
    lanes = channels // LANES
    patches, slope, n1, inv1, n2, inv2 = call(
        lambda *refs: forward_body(rows, width, channels, hidden, block, *refs),
        (place, *close(near, far), *far_off(section_three, dw_kernel, dw_bias, mix_gain, w_expand, w_reduce,
                         layer_scale, down_gain)),
        [SMEM] + [VMEM] * 2 + [HBM] * 8,
        [((band, 4 * channels), BF16), ((count, hidden), F32), ((count, channels), F32),
         ((count, LANES), F32), ((count, channels), F32), ((count, LANES), F32)],
        [pltpu.VMEM((lanes, rows, width, LANES), BF16)] + [pltpu.VMEM(dw_kernel.shape, F32)]
        + [vector] * 4
        + [pltpu.VMEM((lanes, rows + 2 * HALF, width + 2 * LEFT, LANES), F32),
           pltpu.VMEM((count, channels), F32), pltpu.VMEM((count, channels), BF16),
           pltpu.VMEM((count, channels), F32), pltpu.VMEM((lanes, count, LANES), F32),
           pltpu.SemaphoreType.DMA((5,)), pltpu.SemaphoreType.DMA((lanes,))] + weights,
        20, 4 * count * channels * hidden, 9e6,
    )
    held = [patches] + [send(patches, onward(j)) for j in range(1, chips)]
    keep, give, pick, w_near = call(
        lambda *refs: pull_body(spaces, owners, capacity, step, *refs),
        (place, *close(returned), *far_off(owner_table.reshape(1, tokens), w_down)),
        [SMEM, VMEM, HBM, HBM],
        [((chips, band, deep), BF16), ((chips, band, deep), BF16), ((slots, tokens), BF16),
         (w_down.shape, BF16)],
        [pltpu.VMEM((1, tokens), jnp.int32),
         pltpu.VMEM((spaces, band, narrow), BF16), pltpu.VMEM((tokens, narrow), BF16),
         pltpu.SemaphoreType.DMA((1,)), pltpu.SemaphoreType.DMA((deep // step,))],
        12, 2 * tokens * deep * narrow, 4e6,
    )
    sent = send(give, swap)
    sums = call(
        lambda *refs: add_body(chips, *refs),
        (place, *close(keep, sent)), [SMEM, VMEM, VMEM],
        [((band, deep), BF16)] * (chips - 1), [], 4, 2e6, 1e6,
    )
    across = [send(sums[j - 1], onward(j)) for j in range(1, chips)]
    pieces = []
    for piece in held:
        pieces += [piece, send(piece, swap)]
    (buffer,) = call(
        lambda *refs: push_body(chips, *refs),
        (place, *close(*pieces, pick, w_near)),
        [SMEM] + [VMEM] * (len(pieces) + 2),
        [((slots, narrow), BF16)],
        [pltpu.VMEM((tokens, deep), BF16), pltpu.VMEM((spaces, band, narrow), BF16)],
        12, 2 * tokens * deep * narrow, 4e6,
    )
    arrived = trade(buffer)
    (grad_mixed,) = call(
        lambda *refs: backward_body(rows, width, channels, hidden, block, chips, *refs),
        (place, *close(keep, sent, *across, slope, n1, inv1, n2, inv2),
         *far_off(mix_gain, w_expand, w_reduce, layer_scale, down_gain)),
        [SMEM] + [VMEM] * (6 + chips) + [HBM] * 5,
        [jax.ShapeDtypeStruct(section_three.shape, BF16)],
        [vector] * 3
        + [pltpu.VMEM(section_three.shape, BF16), pltpu.VMEM((lanes, count, LANES), F32),
           pltpu.VMEM((count, channels), BF16), pltpu.VMEM((count, channels), F32),
           pltpu.SemaphoreType.DMA((3,)), pltpu.SemaphoreType.DMA((rows,))] + weights,
        16, 4 * count * channels * hidden, 9e6,
    )
    return arrived[None], grad_mixed


def solution(mesh):
    in_specs = (
        P("dp", "space", None, None), P(), P(), P(), P(), P(), P(), P(), P(None, "space"),
        P("dp", None, None), P("dp", None, "space"),
    )
    out_specs = (P("dp", None, "space"), P("dp", "space", None, None))
    return jax.shard_map(
        on_device, mesh=mesh, in_specs=in_specs, out_specs=out_specs, check_vma=False
    )
```

```python
import jax
import jax.numpy as jnp
from jax import lax
from jax.experimental import pallas as pl
from jax.experimental.pallas import tpu as pltpu
from jax.sharding import PartitionSpec as P


KS = 7
HALF = KS // 2
LANES = 128
LEFT = 8
F32 = jnp.float32
BF16 = jnp.bfloat16
VMEM = pl.BlockSpec(memory_space=pltpu.VMEM)
SMEM = pl.BlockSpec(memory_space=pltpu.SMEM)
HBM = pl.BlockSpec(memory_space=pltpu.HBM)


def far_off(*values):
    return tuple(pltpu.with_memory_space_constraint(v, pltpu.HBM) for v in values)


def close(*values):
    return tuple(pltpu.with_memory_space_constraint(v, pltpu.VMEM) for v in values)


def start(copies):
    for copy in copies:
        copy.start()


def wait(copies):
    for copy in copies:
        copy.wait()


def call(body, ins, specs, outs, scratch, limit_mib, flops, moved):
    return pl.pallas_call(
        body,
        in_specs=specs,
        out_shape=tuple(o if isinstance(o, jax.ShapeDtypeStruct) else pltpu.VMEM(*o) for o in outs),
        out_specs=tuple(HBM if isinstance(o, jax.ShapeDtypeStruct) else VMEM for o in outs),
        scratch_shapes=scratch,
        compiler_params=pltpu.CompilerParams(vmem_limit_bytes=limit_mib << 20),
        cost_estimate=pl.CostEstimate(
            flops=int(flops), bytes_accessed=int(moved), transcendentals=0
        ),
    )(*ins)


def nt(a, b):
    return lax.dot_general(a, b, (((1,), (1,)), ((), ())), preferred_element_type=F32)


def nn(a, b):
    return jnp.dot(a, b, preferred_element_type=F32)


def normalize(values):
    center = values - jnp.mean(values, axis=-1, keepdims=True)
    inv_std = lax.rsqrt(jnp.mean(center * center, axis=-1, keepdims=True) + 1e-06)
    return center * inv_std, inv_std


def norm_back(grad, normed, inv_std, gain):
    scaled = grad * gain
    return inv_std * (
        scaled
        - jnp.mean(scaled, axis=-1, keepdims=True)
        - normed * jnp.mean(scaled * normed, axis=-1, keepdims=True)
    )


def fetch(pairs, sems):
    copies = [pltpu.make_async_copy(src, dst, sems.at[i]) for i, (src, dst) in enumerate(pairs)]
    start(copies)
    return copies


def forward_body(
    rows, width, channels, hidden, block,
    place, near_ref, far_ref, x_hbm, kernel_hbm, bias_hbm, gain_hbm, w1_hbm, w2_hbm,
    scale_hbm, down_gain_hbm,
    patch_ref, slope_ref, n1_ref, inv1_ref, n2_ref, inv2_ref,
    x_ref, kernel_ref, bias_ref, gain_ref, scale_ref, down_gain_ref,
    padded, mixed, first, active, acc, grid, small_sems, band_sems, w1_ref, w2_ref, sems,
):
    odd = place[0] % 2 == 1
    chunks = channels // LANES
    tall = rows + 2 * HALF
    sources = (kernel_hbm, bias_hbm, gain_hbm, scale_hbm, down_gain_hbm)
    targets = (kernel_ref, bias_ref, gain_ref, scale_ref, down_gain_ref)
    small = [pltpu.make_async_copy(s, t, small_sems.at[i]) for i, (s, t) in enumerate(zip(sources, targets))]

    def bands(c):
        at = (0, slice(None), slice(None), pl.ds(pl.multiple_of(c * LANES, LANES), LANES))
        return [pltpu.make_async_copy(x_hbm.at[at], x_ref.at[c], band_sems.at[c])]

    start(small[:2])
    for c in range(chunks):
        start(bands(c))
    start(small[2:])
    loads = fetch(((w1_hbm, w1_ref), (w2_hbm, w2_ref)), sems)
    padded[:, :, 0:LEFT, :] = jnp.zeros((chunks, tall, LEFT, LANES), F32)
    padded[:, :, LEFT + width :, :] = jnp.zeros((chunks, tall, LEFT, LANES), F32)
    wait(small[:2])

    def fill(c, _):
        at = pl.ds(pl.multiple_of(c * LANES, LANES), LANES)
        cols = pl.ds(LEFT, width)
        wait(bands(c))
        near, far = near_ref[0, :, :, at].astype(F32), far_ref[0, :, :, at].astype(F32)
        above, below = jnp.where(odd, near, far), jnp.where(odd, far, near)
        padded[c, 0:HALF, cols, :] = above[rows - HALF :]
        padded[c, HALF : HALF + rows, cols, :] = x_ref[c].astype(F32)
        padded[c, HALF + rows :, cols, :] = below[:HALF]
        total = [jnp.zeros((width, LANES), F32) for _ in range(rows)]
        for dx in range(KS):
            taps = [kernel_ref[dy, dx : dx + 1, at] for dy in range(KS)]
            for r in range(tall):
                line = padded[c, r, pl.ds(LEFT - HALF + dx, width), :]
                for out in range(rows):
                    if 0 <= r - out < KS:
                        total[out] = total[out] + line * taps[r - out]
        for out in range(rows):
            mixed[pl.ds(out * width, width), at] = total[out] + bias_ref[at].reshape(1, LANES)
        return 0

    lax.fori_loop(0, chunks, fill, 0)
    wait(small[2:])
    count = rows * width
    step = width
    for r in range(0, count, step):
        n1, inv1 = normalize(mixed[r : r + step, :])
        n1_ref[r : r + step, :] = n1
        inv1_ref[r : r + step, :] = jnp.broadcast_to(inv1, (step, LANES))
        first[r : r + step, :] = (n1 * gain_ref[...].reshape(1, channels)).astype(BF16)
    loads[0].wait()
    for b in range(0, hidden, block):
        pre = nn(first[...], w1_ref[:, b : b + block])
        cumulative = 0.5 * (1.0 + lax.erf(pre * 0.7071067811865476))
        density = jnp.exp(-0.5 * pre * pre) * 0.3989422804014327
        slope_ref[:, b : b + block] = cumulative + pre * density
        active[:, b : b + block] = (pre * cumulative).astype(BF16)
    loads[1].wait()
    for b in range(0, channels, block):
        acc[:, b : b + block] = nn(active[...], w2_ref[:, b : b + block])
    for r in range(rows):
        at = pl.ds(r * width, width)
        line = jnp.concatenate([x_ref[c, r] for c in range(chunks)], axis=1)
        v = line.astype(F32) + scale_ref[...].reshape(1, channels) * acc[at, :]
        n2, inv2 = normalize(v)
        n2_ref[at, :] = n2
        inv2_ref[at, :] = jnp.broadcast_to(inv2, (step, LANES))
        second = n2 * down_gain_ref[...].reshape(1, channels)
        for c in range(chunks):
            grid[c, at, :] = second[:, c * LANES : (c + 1) * LANES]
    half = width // 2
    for r in range(rows // 2):
        for a in range(2):
            for b in range(2):
                piece = jnp.concatenate(
                    [
                        grid[c, pl.ds((2 * r + a) * width + b, half, stride=2), :]
                        for c in range(chunks)
                    ],
                    axis=1,
                )
                patch_ref[r * half : (r + 1) * half, (2 * a + b) * channels : (2 * a + b + 1) * channels] = (
                    piece.astype(BF16)
                )


def pull_body(
    spaces, owners, capacity, step,
    place, returned_ref, table_hbm, w_hbm,
    keep_ref, send_ref, pick_ref, w_ref,
    table_ref, wanted, both, small_sems, sems,
):
    depth = w_ref.shape[0]
    small = [pltpu.make_async_copy(table_hbm, table_ref, small_sems.at[0])]
    start(small)
    loads = []
    for i, d in enumerate(range(0, depth, step)):
        lines = pl.ds(d, step)
        loads.append(pltpu.make_async_copy(w_hbm.at[lines], w_ref.at[lines], sems.at[i]))
        loads[-1].start()
    core = place[0] % 2
    small[0].wait()
    targets = table_ref[...]
    count = targets.shape[1]
    tall = max(owners, 16)
    hot = targets == lax.broadcasted_iota(jnp.int32, (tall, count), 0)
    sooner = lax.broadcasted_iota(jnp.int32, (count, count), 0) < lax.broadcasted_iota(
        jnp.int32, (count, count), 1
    )
    earlier = nn(jnp.where(hot, 1.0, 0.0).astype(BF16), jnp.where(sooner, 1.0, 0.0).astype(BF16))
    rank = jnp.sum(jnp.where(hot, earlier, 0.0), axis=0, keepdims=True).astype(jnp.int32)
    slots = returned_ref.shape[0]
    pick = jnp.where(
        targets * capacity + rank == lax.broadcasted_iota(jnp.int32, (slots, count), 0), 1.0, 0.0
    ).astype(BF16)
    pick_ref[...] = pick
    band = count // spaces
    wanted[...] = (
        lax.dot_general(pick, returned_ref[...], (((0,), (0,)), ((), ())), preferred_element_type=F32)
        .astype(BF16)
        .reshape(wanted.shape)
    )
    chips = spaces // 2
    for i in range(chips):
        both[i * band : (i + 1) * band, :] = wanted[2 * i + core]
        both[(chips + i) * band : (chips + i + 1) * band, :] = wanted[2 * i + 1 - core]
    for n, d in enumerate(range(0, depth, step)):
        loads[n].wait()
        part = nt(both[...], w_ref[d : d + step, :]).astype(BF16)
        for i in range(chips):
            keep_ref[i, :, d : d + step] = part[i * band : (i + 1) * band]
            send_ref[i, :, d : d + step] = part[(chips + i) * band : (chips + i + 1) * band]


def add_body(chips, place, keep_ref, near_ref, *outs):
    chip = place[0] // 2
    for j in range(1, chips):
        at = lax.rem(chip + j, chips)
        outs[j - 1][...] = (keep_ref[at].astype(F32) + near_ref[at].astype(F32)).astype(BF16)


def backward_body(
    rows, width, channels, hidden, block, chips,
    place, keep_ref, near_ref, *rest,
):
    far = rest[: chips - 1]
    (
        slope_ref, n1_ref, inv1_ref, n2_ref, inv2_ref, gain_hbm, w1_hbm, w2_hbm, scale_hbm,
        down_gain_hbm, out_hbm, gain_ref, scale_ref, down_gain_ref, out_ref, grid, scaled, active, acc,
        small_sems, out_sems, w1_ref, w2_ref, sems,
    ) = rest[chips - 1 :]
    sources, targets = (down_gain_hbm, scale_hbm, gain_hbm), (down_gain_ref, scale_ref, gain_ref)
    small = [pltpu.make_async_copy(s, t, small_sems.at[i]) for i, (s, t) in enumerate(zip(sources, targets))]
    start(small)
    loads = fetch(((w2_hbm, w2_ref), (w1_hbm, w1_ref)), sems)
    chip = place[0] // 2
    half = width // 2
    chunks = channels // LANES
    for r in range(rows // 2):
        for a in range(2):
            for b in range(2):
                at = (pl.ds(r * half, half), pl.ds((2 * a + b) * channels, channels))
                value = keep_ref[(chip,) + at].astype(F32) + near_ref[(chip,) + at].astype(F32)
                for piece in far:
                    value = value + piece[at].astype(F32)
                for c in range(chunks):
                    grid[c, pl.ds((2 * r + a) * width + b, half, stride=2), :] = (
                        value[:, c * LANES : (c + 1) * LANES]
                    )
    wait(small)
    for r in range(rows):
        at = pl.ds(r * width, width)
        grad = jnp.concatenate([grid[c, at, :] for c in range(chunks)], axis=1)
        back = norm_back(grad, n2_ref[at, :], inv2_ref[at, 0:1], down_gain_ref[...].reshape(1, channels))
        scaled[at, :] = (back * scale_ref[...].reshape(1, channels)).astype(BF16)
    loads[0].wait()
    for b in range(0, hidden, block):
        active[:, b : b + block] = (nt(scaled[...], w2_ref[b : b + block, :]) * slope_ref[:, b : b + block]).astype(BF16)
    loads[1].wait()
    for b in range(0, channels, block):
        acc[:, b : b + block] = nt(active[...], w1_ref[b : b + block, :])
    stores = []
    for r in range(rows):
        at = pl.ds(r * width, width)
        back = norm_back(acc[at, :], n1_ref[at, :], inv1_ref[at, 0:1], gain_ref[...].reshape(1, channels))
        out_ref[0, r] = back.astype(BF16)
        stores.append(pltpu.make_async_copy(out_ref.at[0, r], out_hbm.at[0, r], out_sems.at[r]))
        stores[-1].start()
    wait(stores)


def push_body(chips, place, *rest):
    pieces = rest[: 2 * chips]
    pick_ref, w_ref, out_ref, patches, tokens = rest[2 * chips :]
    chip, core = place[0] // 2, place[0] % 2
    band = pieces[0].shape[0]
    for i, piece in enumerate(pieces):
        patches[i * band : (i + 1) * band, :] = piece[...]
    result = nn(patches[...], w_ref[...]).astype(BF16)
    for i in range(2 * chips):
        source = lax.rem(chip + chips - i // 2, chips)
        owner = 2 * source + (core if i % 2 == 0 else 1 - core)
        tokens[owner] = result[i * band : (i + 1) * band]
    flat = tokens[...].reshape(2 * chips * band, tokens.shape[2])
    out_ref[...] = nn(pick_ref[...], flat).astype(BF16)


def on_device(
    section_three, dw_kernel, dw_bias, mix_gain, w_expand, w_reduce, layer_scale, down_gain,
    w_down, owner_table, grad_packed,
):
    owners = lax.axis_size("dp")
    spaces = lax.axis_size("space")
    chips = spaces // 2
    slots = grad_packed.shape[1]
    capacity = slots // owners
    _, rows, width, channels = section_three.shape
    hidden = w_expand.shape[1]
    count = rows * width
    band = count // 4
    tokens = owner_table.shape[1]
    deep, narrow = w_down.shape
    place = lax.axis_index("space").astype(jnp.int32).reshape(1)
    block, step = 256, 768
    weights = [
        pltpu.VMEM(w_expand.shape, BF16), pltpu.VMEM(w_reduce.shape, BF16),
        pltpu.SemaphoreType.DMA((2,)),
    ]

    swap = [(i, i ^ 1) for i in range(spaces)]
    joints = [(i, i + 1) for i in range(1, spaces - 1, 2)]
    joints = joints + [(b, a) for a, b in joints]

    def send(value, pairs):
        return lax.ppermute(value, "space", pairs)

    def trade(value):
        return lax.all_to_all(value, "dp", split_axis=0, concat_axis=0, tiled=True)

    def onward(j):
        return [(i, (i + 2 * j) % spaces) for i in range(spaces)]

    near = send(section_three, swap)
    far = send(section_three, joints)
    returned = trade(grad_packed[0])

    vector = pltpu.VMEM((channels,), F32)
    lanes = channels // LANES
    patches, slope, n1, inv1, n2, inv2 = call(
        lambda *refs: forward_body(rows, width, channels, hidden, block, *refs),
        (place, *close(near, far), *far_off(section_three, dw_kernel, dw_bias, mix_gain, w_expand, w_reduce,
                         layer_scale, down_gain)),
        [SMEM] + [VMEM] * 2 + [HBM] * 8,
        [((band, 4 * channels), BF16), ((count, hidden), F32), ((count, channels), F32),
         ((count, LANES), F32), ((count, channels), F32), ((count, LANES), F32)],
        [pltpu.VMEM((lanes, rows, width, LANES), BF16)] + [pltpu.VMEM(dw_kernel.shape, F32)]
        + [vector] * 4
        + [pltpu.VMEM((lanes, rows + 2 * HALF, width + 2 * LEFT, LANES), F32),
           pltpu.VMEM((count, channels), F32), pltpu.VMEM((count, channels), BF16),
           pltpu.VMEM((count, hidden), BF16), pltpu.VMEM((count, channels), F32),
           pltpu.VMEM((lanes, count, LANES), F32),
           pltpu.SemaphoreType.DMA((5,)), pltpu.SemaphoreType.DMA((lanes,))] + weights,
        20, 4 * count * channels * hidden, 9e6,
    )
    held = [patches] + [send(patches, onward(j)) for j in range(1, chips)]
    keep, give, pick, w_near = call(
        lambda *refs: pull_body(spaces, owners, capacity, step, *refs),
        (place, *close(returned), *far_off(owner_table.reshape(1, tokens), w_down)),
        [SMEM, VMEM, HBM, HBM],
        [((chips, band, deep), BF16), ((chips, band, deep), BF16), ((slots, tokens), BF16),
         (w_down.shape, BF16)],
        [pltpu.VMEM((1, tokens), jnp.int32),
         pltpu.VMEM((spaces, band, narrow), BF16), pltpu.VMEM((tokens, narrow), BF16),
         pltpu.SemaphoreType.DMA((1,)), pltpu.SemaphoreType.DMA((deep // step,))],
        12, 2 * tokens * deep * narrow, 4e6,
    )
    sent = send(give, swap)
    sums = call(
        lambda *refs: add_body(chips, *refs),
        (place, *close(keep, sent)), [SMEM, VMEM, VMEM],
        [((band, deep), BF16)] * (chips - 1), [], 4, 2e6, 1e6,
    )
    across = [send(sums[j - 1], onward(j)) for j in range(1, chips)]
    pieces = []
    for piece in held:
        pieces += [piece, send(piece, swap)]
    (buffer,) = call(
        lambda *refs: push_body(chips, *refs),
        (place, *close(*pieces, pick, w_near)),
        [SMEM] + [VMEM] * (len(pieces) + 2),
        [((slots, narrow), BF16)],
        [pltpu.VMEM((tokens, deep), BF16), pltpu.VMEM((spaces, band, narrow), BF16)],
        12, 2 * tokens * deep * narrow, 4e6,
    )
    arrived = trade(buffer)
    (grad_mixed,) = call(
        lambda *refs: backward_body(rows, width, channels, hidden, block, chips, *refs),
        (place, *close(keep, sent, *across, slope, n1, inv1, n2, inv2),
         *far_off(mix_gain, w_expand, w_reduce, layer_scale, down_gain)),
        [SMEM] + [VMEM] * (6 + chips) + [HBM] * 5,
        [jax.ShapeDtypeStruct(section_three.shape, BF16)],
        [vector] * 3
        + [pltpu.VMEM(section_three.shape, BF16), pltpu.VMEM((lanes, count, LANES), F32),
           pltpu.VMEM((count, channels), BF16), pltpu.VMEM((count, hidden), BF16),
           pltpu.VMEM((count, channels), F32), pltpu.SemaphoreType.DMA((3,)), pltpu.SemaphoreType.DMA((rows,))] + weights,
        16, 4 * count * channels * hidden, 9e6,
    )
    return arrived[None], grad_mixed


def solution(mesh):
    in_specs = (
        P("dp", "space", None, None), P(), P(), P(), P(), P(), P(), P(), P(None, "space"),
        P("dp", None, None), P("dp", None, "space"),
    )
    out_specs = (P("dp", None, "space"), P("dp", "space", None, None))
    return jax.shard_map(on_device, mesh=mesh, in_specs=in_specs, out_specs=out_specs, check_vma=False)
```

```python
import jax
import jax.numpy as jnp
from jax import lax
from jax.experimental import pallas as pl
from jax.experimental.pallas import tpu as pltpu
from jax.sharding import PartitionSpec as P


KS = 7
HALF = KS // 2
LANES = 128
LEFT = 8
F32 = jnp.float32
BF16 = jnp.bfloat16
VMEM = pl.BlockSpec(memory_space=pltpu.VMEM)
SMEM = pl.BlockSpec(memory_space=pltpu.SMEM)
HBM = pl.BlockSpec(memory_space=pltpu.HBM)


def far_off(*values):
    return tuple(pltpu.with_memory_space_constraint(v, pltpu.HBM) for v in values)


def close(*values):
    return tuple(pltpu.with_memory_space_constraint(v, pltpu.VMEM) for v in values)


def start(copies):
    for copy in copies:
        copy.start()


def wait(copies):
    for copy in copies:
        copy.wait()


def call(body, ins, specs, outs, scratch, limit_mib, flops, moved):
    return pl.pallas_call(
        body,
        in_specs=specs,
        out_shape=tuple(pltpu.VMEM(*o) if isinstance(o, tuple) else o for o in outs),
        out_specs=tuple(VMEM if isinstance(o, tuple) else HBM for o in outs),
        scratch_shapes=scratch,
        compiler_params=pltpu.CompilerParams(vmem_limit_bytes=limit_mib << 20),
        cost_estimate=pl.CostEstimate(
            flops=int(flops), bytes_accessed=int(moved), transcendentals=0
        ),
    )(*ins)


def nt(a, b):
    return lax.dot_general(a, b, (((1,), (1,)), ((), ())), preferred_element_type=F32)


def nn(a, b):
    return jnp.dot(a, b, preferred_element_type=F32)


def normalize(values):
    center = values - jnp.mean(values, axis=-1, keepdims=True)
    inv_std = lax.rsqrt(jnp.mean(center * center, axis=-1, keepdims=True) + 1e-06)
    return center * inv_std, inv_std


def norm_back(grad, normed, inv_std, gain):
    scaled = grad * gain
    return inv_std * (
        scaled
        - jnp.mean(scaled, axis=-1, keepdims=True)
        - normed * jnp.mean(scaled * normed, axis=-1, keepdims=True)
    )


def fetch(pairs, sems):
    copies = [pltpu.make_async_copy(src, dst, sems.at[i]) for i, (src, dst) in enumerate(pairs)]
    start(copies)
    return copies


def prime_body(out_ref):
    out_ref[...] = jnp.zeros(out_ref.shape, F32)


def forward_body(
    rows, width, channels, hidden, block,
    place, near_ref, far_ref, kernel_ref, bias_ref, gain_ref, scale_ref, down_gain_ref,
    x_hbm, w1_hbm, w2_hbm,
    patch_ref, slope_ref, n1_ref, n2_ref, inv_ref,
    x_ref, padded, mixed, first, active, acc, grid, w1_ref, w2_ref, in_sems,
):
    odd = place[0] % 2 == 1
    chunks = channels // LANES
    tall = rows + 2 * HALF
    loads = fetch(((x_hbm, x_ref), (w1_hbm, w1_ref), (w2_hbm, w2_ref)), in_sems)
    padded[:, :, 0:LEFT, :] = jnp.zeros((chunks, tall, LEFT, LANES), F32)
    padded[:, :, LEFT + width :, :] = jnp.zeros((chunks, tall, LEFT, LANES), F32)
    cols = pl.ds(LEFT, width)
    own = range(HALF, HALF + rows)

    def convolve(c, at, lines, total):
        for dx in range(KS):
            taps = [kernel_ref[dy, dx : dx + 1, at] for dy in range(KS)]
            for r in lines:
                line = padded[c, r, pl.ds(LEFT - HALF + dx, width), :]
                for out in range(rows):
                    if 0 <= r - out < KS:
                        total[out] = total[out] + line * taps[r - out]
        for out in range(rows):
            mixed[pl.ds(out * width, width), at] = total[out]

    def outer(c, _):
        at = pl.ds(pl.multiple_of(c * LANES, LANES), LANES)
        near, far = near_ref[0, :, :, at].astype(F32), far_ref[0, :, :, at].astype(F32)
        above, below = jnp.where(odd, near, far), jnp.where(odd, far, near)
        padded[c, 0:HALF, cols, :] = above[rows - HALF :]
        padded[c, HALF + rows :, cols, :] = below[:HALF]
        bias = jnp.broadcast_to(bias_ref[at].reshape(1, LANES), (width, LANES))
        convolve(c, at, [r for r in range(tall) if r not in own], [bias for _ in range(rows)])
        return 0

    def inner(c, _):
        at = pl.ds(pl.multiple_of(c * LANES, LANES), LANES)
        padded[c, HALF : HALF + rows, cols, :] = x_ref[0, :, :, at].astype(F32)
        convolve(c, at, own, [mixed[pl.ds(out * width, width), at] for out in range(rows)])
        return 0

    lax.fori_loop(0, chunks, outer, 0)
    loads[0].wait()
    lax.fori_loop(0, chunks, inner, 0)
    count = rows * width
    gain = gain_ref[...].reshape(1, channels)
    for r in range(0, count, width):
        n1, inv1 = normalize(mixed[r : r + width, :])
        n1_ref[r : r + width, :] = n1.astype(BF16)
        inv_ref[r : r + width, 0:LANES] = jnp.broadcast_to(inv1, (width, LANES))
        first[r : r + width, :] = (n1 * gain).astype(BF16)
    loads[1].wait()
    for b in range(0, hidden, block):
        pre = nn(first[...], w1_ref[:, b : b + block])
        cumulative = 0.5 * (1.0 + lax.erf(pre * 0.7071067811865476))
        density = jnp.exp(-0.5 * pre * pre) * 0.3989422804014327
        slope_ref[:, b : b + block] = (cumulative + pre * density).astype(BF16)
        active[:, b : b + block] = (pre * cumulative).astype(BF16)
    loads[2].wait()
    for b in range(0, channels, block):
        acc[:, b : b + block] = nn(active[...], w2_ref[:, b : b + block])
    scale, gain = scale_ref[...].reshape(1, channels), down_gain_ref[...].reshape(1, channels)
    for r in range(rows):
        at = pl.ds(r * width, width)
        n2, inv2 = normalize(x_ref[0, r].astype(F32) + scale * acc[at, :])
        n2_ref[at, :] = n2.astype(BF16)
        inv_ref[at, LANES:] = jnp.broadcast_to(inv2, (width, LANES))
        second = n2 * gain
        for c in range(chunks):
            grid[c, at, :] = second[:, c * LANES : (c + 1) * LANES]
    half = width // 2
    for r in range(rows // 2):
        for a in range(2):
            for b in range(2):
                piece = jnp.concatenate(
                    [grid[c, pl.ds((2 * r + a) * width + b, half, stride=2), :] for c in range(chunks)],
                    axis=1,
                )
                patch_ref[r * half : (r + 1) * half, (2 * a + b) * channels : (2 * a + b + 1) * channels] = (
                    piece.astype(BF16)
                )


def index_body(owners, capacity, table_ref, pick_ref):
    targets = table_ref[...]
    slots, count = pick_ref.shape
    tall = max(owners, 16)
    hot = targets == lax.broadcasted_iota(jnp.int32, (tall, count), 0)
    sooner = lax.broadcasted_iota(jnp.int32, (count, count), 0) < lax.broadcasted_iota(
        jnp.int32, (count, count), 1
    )
    earlier = nn(jnp.where(hot, 1.0, 0.0).astype(BF16), jnp.where(sooner, 1.0, 0.0).astype(BF16))
    rank = jnp.sum(jnp.where(hot, earlier, 0.0), axis=0, keepdims=True).astype(jnp.int32)
    pick_ref[...] = jnp.where(
        targets * capacity + rank == lax.broadcasted_iota(jnp.int32, (slots, count), 0), 1.0, 0.0
    ).astype(BF16)


def pull_body(
    spaces, step,
    place, returned_ref, pick_ref, w_hbm, w2_hbm,
    keep_ref, send_ref, w_ref, w2_ref,
    wanted, both, sems,
):
    depth = w_ref.shape[0]
    low, high = pl.ds(0, depth // 2), pl.ds(depth // 2, depth // 2)
    loads = fetch(((w_hbm.at[low], w_ref.at[low]), (w_hbm.at[high], w_ref.at[high])), sems)
    late = pltpu.make_async_copy(w2_hbm.at[pl.ds(0, w2_ref.shape[0])], w2_ref, sems.at[2])
    core = place[0] % 2
    band = both.shape[0] // spaces
    wanted[...] = (
        lax.dot_general(pick_ref[...], returned_ref[...], (((0,), (0,)), ((), ())), preferred_element_type=F32)
        .astype(BF16)
        .reshape(wanted.shape)
    )
    chips = spaces // 2
    for i in range(chips):
        both[i * band : (i + 1) * band, :] = wanted[2 * i + core]
        both[(chips + i) * band : (chips + i + 1) * band, :] = wanted[2 * i + 1 - core]
    for d in range(0, depth, step):
        if d == 0:
            loads[0].wait()
            late.start()
        if d == depth // 2:
            loads[1].wait()
        part = nt(both[...], w_ref[d : d + step, :]).astype(BF16)
        for i in range(chips):
            keep_ref[i, :, d : d + step] = part[i * band : (i + 1) * band]
            send_ref[i, :, d : d + step] = part[(chips + i) * band : (chips + i + 1) * band]
    late.wait()


def add_body(chips, place, keep_ref, near_ref, mine_ref, *outs):
    chip = place[0] // 2
    mine_ref[...] = keep_ref[chip].astype(F32) + near_ref[chip].astype(F32)
    for j in range(1, chips):
        at = lax.rem(chip + j, chips)
        outs[j - 1][...] = (keep_ref[at].astype(F32) + near_ref[at].astype(F32)).astype(BF16)


def backward_body(rows, width, channels, hidden, block, chips, mine_ref, *rest):
    far = rest[: chips - 1]
    (
        slope_ref, n1_ref, n2_ref, inv_ref, w2_near, down_gain_ref, scale_ref, gain_ref, w1_hbm, w2_hbm,
        out_hbm, out_ref, grid, scaled, active, acc, w1_ref, w2_far, in_sems, out_sems,
    ) = rest[chips - 1 :]
    split = w2_near.shape[0]
    loads = fetch(((w2_hbm.at[pl.ds(split, split)], w2_far), (w1_hbm, w1_ref)), in_sems)
    half = width // 2
    chunks = channels // LANES
    for r in range(rows // 2):
        for a in range(2):
            for b in range(2):
                at = (pl.ds(r * half, half), pl.ds((2 * a + b) * channels, channels))
                value = mine_ref[at]
                for piece in far:
                    value = value + piece[at].astype(F32)
                for c in range(chunks):
                    grid[c, pl.ds((2 * r + a) * width + b, half, stride=2), :] = (
                        value[:, c * LANES : (c + 1) * LANES]
                    )
    gain, scale = down_gain_ref[...].reshape(1, channels), scale_ref[...].reshape(1, channels)
    for r in range(rows):
        at = pl.ds(r * width, width)
        grad = jnp.concatenate([grid[c, at, :] for c in range(chunks)], axis=1)
        back = norm_back(grad, n2_ref[at, :].astype(F32), inv_ref[at, LANES : LANES + 1], gain)
        scaled[at, :] = (back * scale).astype(BF16)
    for b in range(0, hidden, block):
        if b == split:
            loads[0].wait()
        weight = w2_near[b : b + block, :] if b < split else w2_far[b - split : b - split + block, :]
        slope = slope_ref[:, b : b + block].astype(F32)
        active[:, b : b + block] = (nt(scaled[...], weight) * slope).astype(BF16)
    loads[1].wait()
    for b in range(0, channels, block):
        acc[:, b : b + block] = nt(active[...], w1_ref[b : b + block, :])
    gain = gain_ref[...].reshape(1, channels)
    stores = []
    for r in range(rows):
        at = pl.ds(r * width, width)
        back = norm_back(acc[at, :], n1_ref[at, :].astype(F32), inv_ref[at, 0:1], gain)
        out_ref[0, r] = back.astype(BF16)
        stores.append(pltpu.make_async_copy(out_ref.at[0, r], out_hbm.at[0, r], out_sems.at[r]))
        stores[-1].start()
    wait(stores)


def push_body(chips, place, *rest):
    pieces = rest[: 2 * chips]
    pick_ref, w_ref, out_ref, patches, tokens = rest[2 * chips :]
    chip, core = place[0] // 2, place[0] % 2
    band = pieces[0].shape[0]
    for i, piece in enumerate(pieces):
        patches[i * band : (i + 1) * band, :] = piece[...]
    result = nn(patches[...], w_ref[...]).astype(BF16)
    for i in range(2 * chips):
        source = lax.rem(chip + chips - i // 2, chips)
        owner = 2 * source + (core if i % 2 == 0 else 1 - core)
        tokens[owner] = result[i * band : (i + 1) * band]
    flat = tokens[...].reshape(2 * chips * band, tokens.shape[2])
    out_ref[...] = nn(pick_ref[...], flat).astype(BF16)


def on_device(
    section_three, dw_kernel, dw_bias, mix_gain, w_expand, w_reduce, layer_scale, down_gain,
    w_down, owner_table, grad_packed,
):
    owners = lax.axis_size("dp")
    spaces = lax.axis_size("space")
    chips = spaces // 2
    slots = grad_packed.shape[1]
    capacity = slots // owners
    _, rows, width, channels = section_three.shape
    hidden = w_expand.shape[1]
    count = rows * width
    band = count // 4
    tokens = owner_table.shape[1]
    deep, narrow = w_down.shape
    place = lax.axis_index("space").astype(jnp.int32).reshape(1)
    lanes = channels // LANES
    block, step = 256, 768

    swap = [(i, i ^ 1) for i in range(spaces)]
    joints = [(i, i + 1) for i in range(1, spaces - 1, 2)]
    joints = joints + [(b, a) for a, b in joints]

    def send(value, pairs):
        return lax.ppermute(value, "space", pairs)

    def trade(value):
        return lax.all_to_all(value, "dp", split_axis=0, concat_axis=0, tiled=True)

    def onward(j):
        return [(i, (i + 2 * j) % spaces) for i in range(spaces)]

    (ready,) = call(prime_body, (), [], [((8, LANES), F32)], [], 1, 5e10, 1e3)
    near = send(section_three, swap)
    far = send(section_three, joints)
    returned = trade(grad_packed[0])

    patches, slope, n1, n2, inv = call(
        lambda *refs: forward_body(rows, width, channels, hidden, block, *refs[:8], *refs[9:]),
        (place, *close(near, far, dw_kernel, dw_bias, mix_gain, layer_scale, down_gain, ready),
         *far_off(section_three, w_expand, w_reduce)),
        [SMEM] + [VMEM] * 8 + [HBM] * 3,
        [((band, 4 * channels), BF16), ((count, hidden), BF16), ((count, channels), BF16),
         ((count, channels), BF16), ((count, 2 * LANES), F32)],
        [pltpu.VMEM(section_three.shape, BF16),
         pltpu.VMEM((lanes, rows + 2 * HALF, width + 2 * LEFT, LANES), F32),
         pltpu.VMEM((count, channels), F32), pltpu.VMEM((count, channels), BF16),
         pltpu.VMEM((count, hidden), BF16), pltpu.VMEM((count, channels), F32),
         pltpu.VMEM((lanes, count, LANES), F32),
         pltpu.VMEM(w_expand.shape, BF16), pltpu.VMEM(w_reduce.shape, BF16),
         pltpu.SemaphoreType.DMA((3,))],
        20, 4 * count * channels * hidden, 9e6,
    )
    held = [patches] + [send(patches, onward(j)) for j in range(1, chips)]
    (pick,) = call(
        lambda *refs: index_body(owners, capacity, *refs),
        close(owner_table.reshape(1, tokens)), [VMEM],
        [((slots, tokens), BF16)], [], 2, 1e7, 1e5,
    )
    keep, give, w_near, w2_near = call(
        lambda *refs: pull_body(spaces, step, *refs),
        (place, *close(returned, pick), *far_off(w_down, w_reduce)),
        [SMEM] + [VMEM] * 2 + [HBM] * 2,
        [((chips, band, deep), BF16), ((chips, band, deep), BF16), (w_down.shape, BF16),
         ((hidden // 2, channels), BF16)],
        [pltpu.VMEM((spaces, band, narrow), BF16), pltpu.VMEM((tokens, narrow), BF16),
         pltpu.SemaphoreType.DMA((3,))],
        6, 2 * tokens * deep * narrow, 4e6,
    )
    sent = send(give, swap)
    mine, *sums = call(
        lambda *refs: add_body(chips, *refs),
        (place, *close(keep, sent)), [SMEM, VMEM, VMEM],
        [((band, deep), F32)] + [((band, deep), BF16)] * (chips - 1), [], 4, 2e6, 1e6,
    )
    across = [send(sums[j - 1], onward(j)) for j in range(1, chips)]
    pieces = []
    for piece in held:
        pieces += [piece, send(piece, swap)]
    (buffer,) = call(
        lambda *refs: push_body(chips, *refs),
        (place, *close(*pieces, pick, w_near)),
        [SMEM] + [VMEM] * (len(pieces) + 2),
        [((slots, narrow), BF16)],
        [pltpu.VMEM((tokens, deep), BF16), pltpu.VMEM((spaces, band, narrow), BF16)],
        6, 2 * tokens * deep * narrow, 4e6,
    )
    arrived = trade(buffer)
    (grad_mixed,) = call(
        lambda *refs: backward_body(rows, width, channels, hidden, block, chips, *refs),
        (*close(mine, *across, slope, n1, n2, inv, w2_near, down_gain, layer_scale, mix_gain),
         *far_off(w_expand, w_reduce)),
        [VMEM] * (8 + chips) + [HBM] * 2,
        [jax.ShapeDtypeStruct(section_three.shape, BF16)],
        [pltpu.VMEM(section_three.shape, BF16), pltpu.VMEM((lanes, count, LANES), F32),
         pltpu.VMEM((count, channels), BF16), pltpu.VMEM((count, hidden), BF16),
         pltpu.VMEM((count, channels), F32),
         pltpu.VMEM(w_expand.shape, BF16), pltpu.VMEM((hidden // 2, channels), BF16),
         pltpu.SemaphoreType.DMA((2,)), pltpu.SemaphoreType.DMA((rows,))],
        16, 4 * count * channels * hidden, 9e6,
    )
    return arrived[None], grad_mixed


def solution(mesh):
    in_specs = (
        P("dp", "space", None, None), P(), P(), P(), P(), P(), P(), P(), P(None, "space"),
        P("dp", None, None), P("dp", None, "space"),
    )
    out_specs = (P("dp", None, "space"), P("dp", "space", None, None))
    return jax.shard_map(
        on_device, mesh=mesh, in_specs=in_specs, out_specs=out_specs, check_vma=False
    )
```

```python
import jax
import jax.numpy as jnp
from jax import lax
from jax.experimental import pallas as pl
from jax.experimental.pallas import tpu as pltpu
from jax.sharding import PartitionSpec as P


KS = 7
HALF = KS // 2
LANES = 128
LEFT = 8
F32 = jnp.float32
BF16 = jnp.bfloat16
VMEM = pl.BlockSpec(memory_space=pltpu.VMEM)
SMEM = pl.BlockSpec(memory_space=pltpu.SMEM)
HBM = pl.BlockSpec(memory_space=pltpu.HBM)


def far_off(*values):
    return tuple(pltpu.with_memory_space_constraint(v, pltpu.HBM) for v in values)


def close(*values):
    return tuple(pltpu.with_memory_space_constraint(v, pltpu.VMEM) for v in values)


def start(copies):
    for copy in copies:
        copy.start()


def wait(copies):
    for copy in copies:
        copy.wait()


def call(body, ins, specs, outs, scratch, limit_mib, flops, moved):
    return pl.pallas_call(
        body,
        in_specs=specs,
        out_shape=tuple(pltpu.VMEM(*o) if isinstance(o, tuple) else o for o in outs),
        out_specs=tuple(VMEM if isinstance(o, tuple) else HBM for o in outs),
        scratch_shapes=scratch,
        compiler_params=pltpu.CompilerParams(vmem_limit_bytes=limit_mib << 20),
        cost_estimate=pl.CostEstimate(
            flops=int(flops), bytes_accessed=int(moved), transcendentals=0
        ),
    )(*ins)


def nt(a, b):
    return lax.dot_general(a, b, (((1,), (1,)), ((), ())), preferred_element_type=F32)


def nn(a, b):
    return jnp.dot(a, b, preferred_element_type=F32)


def normalize(values):
    center = values - jnp.mean(values, axis=-1, keepdims=True)
    inv_std = lax.rsqrt(jnp.mean(center * center, axis=-1, keepdims=True) + 1e-06)
    return center * inv_std, inv_std


def norm_back(grad, normed, inv_std, gain):
    scaled = grad * gain
    return inv_std * (
        scaled
        - jnp.mean(scaled, axis=-1, keepdims=True)
        - normed * jnp.mean(scaled * normed, axis=-1, keepdims=True)
    )


def fetch(pairs, sems):
    copies = [pltpu.make_async_copy(src, dst, sems.at[i]) for i, (src, dst) in enumerate(pairs)]
    start(copies)
    return copies


def prime_body(out_ref):
    out_ref[...] = jnp.zeros(out_ref.shape, F32)


def convolve(padded, c, first_line, lines, total, kernel_ref, at, rows, width):
    for dx in range(KS):
        taps = [kernel_ref[dy, dx : dx + 1, at] for dy in range(KS)]
        for r in lines:
            line = padded[c, first_line(r), pl.ds(LEFT - HALF + dx, width), :]
            for out in range(rows):
                if 0 <= r - out < KS:
                    total[out] = total[out] + line * taps[r - out]
    return total


def conv_body(rows, width, channels, chips, kernel_ref, bias_ref, ready, *rest):
    bands, (w1_hbm, w2_hbm, part_ref, w1_ref, w2_ref, padded, sems) = rest[:chips], rest[chips:]
    loads = fetch(((w1_hbm, w1_ref), (w2_hbm, w2_ref)), sems)
    chunks = channels // LANES
    cols = pl.ds(LEFT, width)
    padded[:, :, 0:LEFT, :] = jnp.zeros((chunks, rows, LEFT, LANES), F32)
    padded[:, :, LEFT + width :, :] = jnp.zeros((chunks, rows, LEFT, LANES), F32)
    for q, band_ref in enumerate(bands):

        def own(c, _):
            at = pl.ds(pl.multiple_of(c * LANES, LANES), LANES)
            padded[c, :, cols, :] = band_ref[0, :, :, at].astype(F32)
            bias = jnp.broadcast_to(bias_ref[at].reshape(1, LANES), (width, LANES))
            lines = range(HALF, HALF + rows)
            total = convolve(padded, c, lambda r: r - HALF, lines, [bias] * rows, kernel_ref, at, rows, width)
            for out in range(rows):
                part_ref[pl.ds((q * rows + out) * width, width), at] = total[out]
            return 0

        lax.fori_loop(0, chunks, own, 0)
    wait(loads)


def forward_body(rows, width, channels, hidden, block, chips, place, part_ref, kernel_ref, *rest):
    mates, bands = rest[:chips], rest[chips : 2 * chips]
    (
        gain_ref, scale_ref, down_gain_ref, w1_ref, w2_ref,
        patch_ref, slope_ref, n1_ref, n2_ref, inv_ref,
        padded, mixed, first, active, acc, grid,
    ) = rest[2 * chips :]
    chip, odd = place[0] // 2, place[0] % 2 == 1
    chunks = channels // LANES
    count = rows * width
    cols = pl.ds(LEFT, width)
    padded[:, :, 0:LEFT, :] = jnp.zeros((chunks, 2 * HALF, LEFT, LANES), F32)
    padded[:, :, LEFT + width :, :] = jnp.zeros((chunks, 2 * HALF, LEFT, LANES), F32)
    for q in range(chips):
        level = lax.rem(chip + chips - q, chips)
        same, over, under = mates[q], mates[(q + 1) % chips], mates[(q - 1) % chips]

        def outer(c, _):
            at = pl.ds(pl.multiple_of(c * LANES, LANES), LANES)
            low, high = slice(0, HALF), slice(rows - HALF, rows)
            above = jnp.where(level > 0, over[0, high, :, at].astype(F32), 0.0)
            below = jnp.where(level < chips - 1, under[0, low, :, at].astype(F32), 0.0)
            padded[c, 0:HALF, cols, :] = jnp.where(odd, same[0, high, :, at].astype(F32), above)
            padded[c, HALF:, cols, :] = jnp.where(odd, below, same[0, low, :, at].astype(F32))
            spots = [pl.ds((q * rows + out) * width, width) for out in range(rows)]
            lines = [r for r in range(rows + 2 * HALF) if not HALF <= r < HALF + rows]
            total = convolve(
                padded, c, lambda r: r if r < HALF else r - rows, lines, [part_ref[p, at] for p in spots],
                kernel_ref, at, rows, width,
            )
            for p, value in zip(spots, total):
                mixed[p, at] = value
            return 0

        lax.fori_loop(0, chunks, outer, 0)
    gain = gain_ref[...].reshape(1, channels)
    for r in range(0, chips * count, width):
        n1, inv1 = normalize(mixed[r : r + width, :])
        if r < count:
            n1_ref[r : r + width, :] = n1.astype(BF16)
            inv_ref[r : r + width, 0:LANES] = jnp.broadcast_to(inv1, (width, LANES))
        first[r : r + width, :] = (n1 * gain).astype(BF16)
    for b in range(0, hidden, block):
        pre = nn(first[...], w1_ref[:, b : b + block])
        cumulative = 0.5 * (1.0 + lax.erf(pre * 0.7071067811865476))
        mine = pre[:count]
        density = jnp.exp(-0.5 * mine * mine) * 0.3989422804014327
        slope_ref[:, b : b + block] = (cumulative[:count] + mine * density).astype(BF16)
        active[:, b : b + block] = (pre * cumulative).astype(BF16)
    for b in range(0, channels, block):
        acc[:, b : b + block] = nn(active[...], w2_ref[:, b : b + block])
    scale, gain = scale_ref[...].reshape(1, channels), down_gain_ref[...].reshape(1, channels)
    half = width // 2
    for q in range(chips):
        for r in range(rows):
            at = pl.ds(r * width, width)
            n2, inv2 = normalize(bands[q][0, r].astype(F32) + scale * acc[pl.ds(q * count + r * width, width), :])
            if q == 0:
                n2_ref[at, :] = n2.astype(BF16)
                inv_ref[at, LANES:] = jnp.broadcast_to(inv2, (width, LANES))
            second = n2 * gain
            for c in range(chunks):
                grid[c, pl.ds(q * count + r * width, width), :] = second[:, c * LANES : (c + 1) * LANES]
        for r in range(rows // 2):
            for a in range(2):
                for b in range(2):
                    spot = pl.ds(q * count + (2 * r + a) * width + b, half, stride=2)
                    piece = jnp.concatenate([grid[c, spot, :] for c in range(chunks)], axis=1)
                    patch_ref[q, r * half : (r + 1) * half, (2 * a + b) * channels : (2 * a + b + 1) * channels] = (
                        piece.astype(BF16)
                    )


def index_body(owners, capacity, table_ref, pick_ref):
    targets = table_ref[...]
    slots, count = pick_ref.shape
    tall = max(owners, 16)
    hot = targets == lax.broadcasted_iota(jnp.int32, (tall, count), 0)
    sooner = lax.broadcasted_iota(jnp.int32, (count, count), 0) < lax.broadcasted_iota(
        jnp.int32, (count, count), 1
    )
    earlier = nn(jnp.where(hot, 1.0, 0.0).astype(BF16), jnp.where(sooner, 1.0, 0.0).astype(BF16))
    rank = jnp.sum(jnp.where(hot, earlier, 0.0), axis=0, keepdims=True).astype(jnp.int32)
    pick_ref[...] = jnp.where(
        targets * capacity + rank == lax.broadcasted_iota(jnp.int32, (slots, count), 0), 1.0, 0.0
    ).astype(BF16)


def pull_body(
    spaces, step,
    place, returned_ref, pick_ref, w_hbm, w2_hbm,
    keep_ref, send_ref, w_ref, w2_ref,
    wanted, both, sems,
):
    depth = w_ref.shape[0]
    low, high = pl.ds(0, depth // 2), pl.ds(depth // 2, depth // 2)
    loads = fetch(((w_hbm.at[low], w_ref.at[low]), (w_hbm.at[high], w_ref.at[high])), sems)
    late = pltpu.make_async_copy(w2_hbm.at[pl.ds(0, w2_ref.shape[0])], w2_ref, sems.at[2])
    core = place[0] % 2
    band = both.shape[0] // spaces
    wanted[...] = (
        lax.dot_general(pick_ref[...], returned_ref[...], (((0,), (0,)), ((), ())), preferred_element_type=F32)
        .astype(BF16)
        .reshape(wanted.shape)
    )
    chips = spaces // 2
    for i in range(chips):
        both[i * band : (i + 1) * band, :] = wanted[2 * i + core]
        both[(chips + i) * band : (chips + i + 1) * band, :] = wanted[2 * i + 1 - core]
    for d in range(0, depth, step):
        if d == 0:
            loads[0].wait()
            late.start()
        if d == depth // 2:
            loads[1].wait()
        part = nt(both[...], w_ref[d : d + step, :]).astype(BF16)
        for i in range(chips):
            keep_ref[i, :, d : d + step] = part[i * band : (i + 1) * band]
            send_ref[i, :, d : d + step] = part[(chips + i) * band : (chips + i + 1) * band]
    late.wait()


def add_body(chips, place, keep_ref, near_ref, mine_ref, *outs):
    chip = place[0] // 2
    mine_ref[...] = keep_ref[chip].astype(F32) + near_ref[chip].astype(F32)
    for j in range(1, chips):
        at = lax.rem(chip + j, chips)
        outs[j - 1][...] = (keep_ref[at].astype(F32) + near_ref[at].astype(F32)).astype(BF16)


def backward_body(rows, width, channels, hidden, block, chips, mine_ref, *rest):
    far = rest[: chips - 1]
    (
        slope_ref, n1_ref, n2_ref, inv_ref, w2_near, down_gain_ref, scale_ref, gain_ref, w1_hbm, w2_hbm,
        out_hbm, out_ref, grid, scaled, active, acc, w1_ref, w2_far, in_sems, out_sems,
    ) = rest[chips - 1 :]
    split = w2_near.shape[0]
    loads = fetch(((w2_hbm.at[pl.ds(split, split)], w2_far), (w1_hbm, w1_ref)), in_sems)
    half = width // 2
    chunks = channels // LANES
    for r in range(rows // 2):
        for a in range(2):
            for b in range(2):
                at = (pl.ds(r * half, half), pl.ds((2 * a + b) * channels, channels))
                value = mine_ref[at]
                for piece in far:
                    value = value + piece[at].astype(F32)
                for c in range(chunks):
                    grid[c, pl.ds((2 * r + a) * width + b, half, stride=2), :] = (
                        value[:, c * LANES : (c + 1) * LANES]
                    )
    gain, scale = down_gain_ref[...].reshape(1, channels), scale_ref[...].reshape(1, channels)
    for r in range(rows):
        at = pl.ds(r * width, width)
        grad = jnp.concatenate([grid[c, at, :] for c in range(chunks)], axis=1)
        back = norm_back(grad, n2_ref[at, :].astype(F32), inv_ref[at, LANES : LANES + 1], gain)
        scaled[at, :] = (back * scale).astype(BF16)
    for b in range(0, hidden, block):
        if b == split:
            loads[0].wait()
        weight = w2_near[b : b + block, :] if b < split else w2_far[b - split : b - split + block, :]
        slope = slope_ref[:, b : b + block].astype(F32)
        active[:, b : b + block] = (nt(scaled[...], weight) * slope).astype(BF16)
    loads[1].wait()
    for b in range(0, channels, block):
        acc[:, b : b + block] = nt(active[...], w1_ref[b : b + block, :])
    gain = gain_ref[...].reshape(1, channels)
    stores = []
    for r in range(rows):
        at = pl.ds(r * width, width)
        back = norm_back(acc[at, :], n1_ref[at, :].astype(F32), inv_ref[at, 0:1], gain)
        out_ref[0, r] = back.astype(BF16)
        stores.append(pltpu.make_async_copy(out_ref.at[0, r], out_hbm.at[0, r], out_sems.at[r]))
        stores[-1].start()
    wait(stores)


def push_body(chips, place, own_ref, mate_ref, pick_ref, w_ref, out_ref, patches, tokens):
    chip, core = place[0] // 2, place[0] % 2
    band = own_ref.shape[1]
    for i in range(2 * chips):
        source_ref = own_ref if i % 2 == 0 else mate_ref
        patches[i * band : (i + 1) * band, :] = source_ref[i // 2]
    result = nn(patches[...], w_ref[...]).astype(BF16)
    for i in range(2 * chips):
        source = lax.rem(chip + chips - i // 2, chips)
        owner = 2 * source + (core if i % 2 == 0 else 1 - core)
        tokens[owner] = result[i * band : (i + 1) * band]
    flat = tokens[...].reshape(2 * chips * band, tokens.shape[2])
    out_ref[...] = nn(pick_ref[...], flat).astype(BF16)


def on_device(
    section_three, dw_kernel, dw_bias, mix_gain, w_expand, w_reduce, layer_scale, down_gain,
    w_down, owner_table, grad_packed,
):
    owners = lax.axis_size("dp")
    spaces = lax.axis_size("space")
    chips = spaces // 2
    slots = grad_packed.shape[1]
    capacity = slots // owners
    _, rows, width, channels = section_three.shape
    hidden = w_expand.shape[1]
    count = rows * width
    band = count // 4
    tokens = owner_table.shape[1]
    deep, narrow = w_down.shape
    place = lax.axis_index("space").astype(jnp.int32).reshape(1)
    lanes = channels // LANES
    block, step = 256, 768

    swap = [(i, i ^ 1) for i in range(spaces)]

    def send(value, pairs):
        return lax.ppermute(value, "space", pairs)

    def trade(value):
        return lax.all_to_all(value, "dp", split_axis=0, concat_axis=0, tiled=True)

    def onward(j):
        return [(i, (i + 2 * j) % spaces) for i in range(spaces)]

    (ready,) = call(prime_body, (), [], [((8, LANES), F32)], [], 1, 5e10, 1e3)
    near = send(section_three, swap)
    bands = [section_three] + [send(section_three, onward(j)) for j in range(1, chips)]
    returned = trade(grad_packed[0])

    mates = [near] + [send(bands[j], swap) for j in range(1, chips)]
    wide = chips * count
    part, w1_near, w2_whole = call(
        lambda *refs: conv_body(rows, width, channels, chips, *refs),
        (*close(dw_kernel, dw_bias, ready, *bands), *far_off(w_expand, w_reduce)),
        [VMEM] * (3 + chips) + [HBM] * 2,
        [((wide, channels), F32), (w_expand.shape, BF16), (w_reduce.shape, BF16)],
        [pltpu.VMEM((lanes, rows, width + 2 * LEFT, LANES), F32), pltpu.SemaphoreType.DMA((2,))],
        6, 4e9, 6e6,
    )
    patches, slope, n1, n2, inv = call(
        lambda *refs: forward_body(rows, width, channels, hidden, block, chips, *refs),
        (place, *close(part, dw_kernel, *mates, *bands, mix_gain, layer_scale, down_gain, w1_near, w2_whole)),
        [SMEM] + [VMEM] * (7 + 2 * chips),
        [((chips, band, 4 * channels), BF16), ((count, hidden), BF16), ((count, channels), BF16),
         ((count, channels), BF16), ((count, 2 * LANES), F32)],
        [pltpu.VMEM((lanes, 2 * HALF, width + 2 * LEFT, LANES), F32),
         pltpu.VMEM((wide, channels), F32), pltpu.VMEM((wide, channels), BF16),
         pltpu.VMEM((wide, hidden), BF16), pltpu.VMEM((wide, channels), F32),
         pltpu.VMEM((lanes, wide, LANES), F32)],
        20, 4 * wide * channels * hidden, 9e6,
    )
    mate_patches = send(patches, swap)
    (pick,) = call(
        lambda *refs: index_body(owners, capacity, *refs),
        close(owner_table.reshape(1, tokens)), [VMEM],
        [((slots, tokens), BF16)], [], 2, 1e7, 1e5,
    )
    keep, give, w_near, w2_near = call(
        lambda *refs: pull_body(spaces, step, *refs),
        (place, *close(returned, pick), *far_off(w_down, w_reduce)),
        [SMEM] + [VMEM] * 2 + [HBM] * 2,
        [((chips, band, deep), BF16), ((chips, band, deep), BF16), (w_down.shape, BF16),
         ((hidden // 2, channels), BF16)],
        [pltpu.VMEM((spaces, band, narrow), BF16), pltpu.VMEM((tokens, narrow), BF16),
         pltpu.SemaphoreType.DMA((3,))],
        6, 2 * tokens * deep * narrow, 4e6,
    )
    sent = send(give, swap)
    mine, *sums = call(
        lambda *refs: add_body(chips, *refs),
        (place, *close(keep, sent)), [SMEM, VMEM, VMEM],
        [((band, deep), F32)] + [((band, deep), BF16)] * (chips - 1), [], 4, 2e6, 1e6,
    )
    across = [send(sums[j - 1], onward(j)) for j in range(1, chips)]
    (buffer,) = call(
        lambda *refs: push_body(chips, *refs),
        (place, *close(patches, mate_patches, pick, w_near)),
        [SMEM] + [VMEM] * 4,
        [((slots, narrow), BF16)],
        [pltpu.VMEM((tokens, deep), BF16), pltpu.VMEM((spaces, band, narrow), BF16)],
        6, 2 * tokens * deep * narrow, 4e6,
    )
    arrived = trade(buffer)
    (grad_mixed,) = call(
        lambda *refs: backward_body(rows, width, channels, hidden, block, chips, *refs),
        (*close(mine, *across, slope, n1, n2, inv, w2_near, down_gain, layer_scale, mix_gain),
         *far_off(w_expand, w_reduce)),
        [VMEM] * (8 + chips) + [HBM] * 2,
        [jax.ShapeDtypeStruct(section_three.shape, BF16)],
        [pltpu.VMEM(section_three.shape, BF16), pltpu.VMEM((lanes, count, LANES), F32),
         pltpu.VMEM((count, channels), BF16), pltpu.VMEM((count, hidden), BF16),
         pltpu.VMEM((count, channels), F32),
         pltpu.VMEM(w_expand.shape, BF16), pltpu.VMEM((hidden // 2, channels), BF16),
         pltpu.SemaphoreType.DMA((2,)), pltpu.SemaphoreType.DMA((rows,))],
        16, 4 * count * channels * hidden, 9e6,
    )
    return arrived[None], grad_mixed


def solution(mesh):
    in_specs = (
        P("dp", "space", None, None), P(), P(), P(), P(), P(), P(), P(), P(None, "space"),
        P("dp", None, None), P("dp", None, "space"),
    )
    out_specs = (P("dp", None, "space"), P("dp", "space", None, None))
    return jax.shard_map(on_device, mesh=mesh, in_specs=in_specs, out_specs=out_specs, check_vma=False)
```

```python
import jax
import jax.numpy as jnp
from jax import lax
from jax.experimental import pallas as pl
from jax.experimental.pallas import tpu as pltpu
from jax.sharding import PartitionSpec as P


KS = 7
HALF = KS // 2
LANES = 128
LEFT = 8
F32 = jnp.float32
BF16 = jnp.bfloat16
VMEM = pl.BlockSpec(memory_space=pltpu.VMEM)
SMEM = pl.BlockSpec(memory_space=pltpu.SMEM)
HBM = pl.BlockSpec(memory_space=pltpu.HBM)


def far_off(*values):
    return tuple(pltpu.with_memory_space_constraint(v, pltpu.HBM) for v in values)


def close(*values):
    return tuple(pltpu.with_memory_space_constraint(v, pltpu.VMEM) for v in values)


def start(copies):
    for copy in copies:
        copy.start()


def wait(copies):
    for copy in copies:
        copy.wait()


def call(body, ins, specs, outs, scratch, limit_mib, flops, moved):
    return pl.pallas_call(
        body,
        in_specs=specs,
        out_shape=tuple(pltpu.VMEM(*o) if isinstance(o, tuple) else o for o in outs),
        out_specs=tuple(VMEM if isinstance(o, tuple) else HBM for o in outs),
        scratch_shapes=scratch,
        compiler_params=pltpu.CompilerParams(vmem_limit_bytes=limit_mib << 20),
        cost_estimate=pl.CostEstimate(
            flops=int(flops), bytes_accessed=int(moved), transcendentals=0
        ),
    )(*ins)


def nt(a, b):
    return lax.dot_general(a, b, (((1,), (1,)), ((), ())), preferred_element_type=F32)


def nn(a, b):
    return jnp.dot(a, b, preferred_element_type=F32)


def normalize(values):
    center = values - jnp.mean(values, axis=-1, keepdims=True)
    inv_std = lax.rsqrt(jnp.mean(center * center, axis=-1, keepdims=True) + 1e-06)
    return center * inv_std, inv_std


def norm_back(grad, normed, inv_std, gain):
    scaled = grad * gain
    return inv_std * (
        scaled
        - jnp.mean(scaled, axis=-1, keepdims=True)
        - normed * jnp.mean(scaled * normed, axis=-1, keepdims=True)
    )


def fetch(pairs, sems):
    copies = [pltpu.make_async_copy(src, dst, sems.at[i]) for i, (src, dst) in enumerate(pairs)]
    start(copies)
    return copies


def prime_body(out_ref):
    out_ref[...] = jnp.zeros(out_ref.shape, F32)


def convolve(padded, c, first_line, lines, total, kernel_ref, at, rows, width):
    for dx in range(KS):
        taps = [kernel_ref[dy, dx : dx + 1, at] for dy in range(KS)]
        for r in lines:
            line = padded[c, first_line(r), pl.ds(LEFT - HALF + dx, width), :]
            for out in range(rows):
                if 0 <= r - out < KS:
                    total[out] = total[out] + line * taps[r - out]
    return total


def conv_body(rows, width, channels, chips, kernel_ref, bias_ref, ready, *rest):
    bands, (w1_hbm, w2_hbm, part_ref, w1_ref, w2_ref, padded, sems) = rest[:chips], rest[chips:]
    loads = fetch(((w1_hbm, w1_ref), (w2_hbm, w2_ref)), sems)
    chunks = channels // LANES
    cols = pl.ds(LEFT, width)
    padded[:, :, 0:LEFT, :] = jnp.zeros((chunks, rows, LEFT, LANES), F32)
    padded[:, :, LEFT + width :, :] = jnp.zeros((chunks, rows, LEFT, LANES), F32)
    for q, band_ref in enumerate(bands):

        def own(c, _):
            at = pl.ds(pl.multiple_of(c * LANES, LANES), LANES)
            padded[c, :, cols, :] = band_ref[0, :, :, at].astype(F32)
            bias = jnp.broadcast_to(bias_ref[at].reshape(1, LANES), (width, LANES))
            lines = range(HALF, HALF + rows)
            total = convolve(padded, c, lambda r: r - HALF, lines, [bias] * rows, kernel_ref, at, rows, width)
            for out in range(rows):
                part_ref[pl.ds((q * rows + out) * width, width), at] = total[out]
            return 0

        lax.fori_loop(0, chunks, own, 0)
    wait(loads)


def forward_body(rows, width, channels, hidden, block, chips, place, part_ref, kernel_ref, *rest):
    mates, bands = rest[:chips], rest[chips : 2 * chips]
    (
        gain_ref, scale_ref, down_gain_ref, w1_ref, w2_ref, w3_hbm,
        patch_ref, slope_ref, n1_ref, n2_ref, inv_ref, w3_ref,
        padded, mixed, first, active, acc, grid, sems,
    ) = rest[2 * chips :]
    loads = fetch(((w3_hbm.at[pl.ds(0, w3_ref.shape[0])], w3_ref),), sems)
    chip, odd = place[0] // 2, place[0] % 2 == 1
    chunks = channels // LANES
    count = rows * width
    cols = pl.ds(LEFT, width)
    padded[:, :, 0:LEFT, :] = jnp.zeros((chunks, 2 * HALF, LEFT, LANES), F32)
    padded[:, :, LEFT + width :, :] = jnp.zeros((chunks, 2 * HALF, LEFT, LANES), F32)
    for q in range(chips):
        level = lax.rem(chip + chips - q, chips)
        same, over, under = mates[q], mates[(q + 1) % chips], mates[(q - 1) % chips]

        def outer(c, _):
            at = pl.ds(pl.multiple_of(c * LANES, LANES), LANES)
            low, high = slice(0, HALF), slice(rows - HALF, rows)
            above = jnp.where(level > 0, over[0, high, :, at].astype(F32), 0.0)
            below = jnp.where(level < chips - 1, under[0, low, :, at].astype(F32), 0.0)
            padded[c, 0:HALF, cols, :] = jnp.where(odd, same[0, high, :, at].astype(F32), above)
            padded[c, HALF:, cols, :] = jnp.where(odd, below, same[0, low, :, at].astype(F32))
            spots = [pl.ds((q * rows + out) * width, width) for out in range(rows)]
            lines = [r for r in range(rows + 2 * HALF) if not HALF <= r < HALF + rows]
            total = convolve(
                padded, c, lambda r: r if r < HALF else r - rows, lines, [part_ref[p, at] for p in spots],
                kernel_ref, at, rows, width,
            )
            for p, value in zip(spots, total):
                mixed[p, at] = value
            return 0

        lax.fori_loop(0, chunks, outer, 0)
    gain = gain_ref[...].reshape(1, channels)
    for r in range(0, chips * count, width):
        n1, inv1 = normalize(mixed[r : r + width, :])
        if r < count:
            n1_ref[r : r + width, :] = n1.astype(BF16)
            inv_ref[r : r + width, 0:LANES] = jnp.broadcast_to(inv1, (width, LANES))
        first[r : r + width, :] = (n1 * gain).astype(BF16)
    for b in range(0, hidden, block):
        pre = nn(first[...], w1_ref[:, b : b + block])
        cumulative = 0.5 * (1.0 + lax.erf(pre * 0.7071067811865476))
        mine = pre[:count]
        density = jnp.exp(-0.5 * mine * mine) * 0.3989422804014327
        slope_ref[:, b : b + block] = (cumulative[:count] + mine * density).astype(BF16)
        active[:, b : b + block] = (pre * cumulative).astype(BF16)
    for b in range(0, channels, block):
        acc[:, b : b + block] = nn(active[...], w2_ref[:, b : b + block])
    scale, gain = scale_ref[...].reshape(1, channels), down_gain_ref[...].reshape(1, channels)
    half = width // 2
    for q in range(chips):
        for r in range(rows):
            at = pl.ds(r * width, width)
            n2, inv2 = normalize(bands[q][0, r].astype(F32) + scale * acc[pl.ds(q * count + r * width, width), :])
            if q == 0:
                n2_ref[at, :] = n2.astype(BF16)
                inv_ref[at, LANES:] = jnp.broadcast_to(inv2, (width, LANES))
            second = n2 * gain
            for c in range(chunks):
                grid[c, pl.ds(q * count + r * width, width), :] = second[:, c * LANES : (c + 1) * LANES]
        for r in range(rows // 2):
            for a in range(2):
                for b in range(2):
                    spot = pl.ds(q * count + (2 * r + a) * width + b, half, stride=2)
                    piece = jnp.concatenate([grid[c, spot, :] for c in range(chunks)], axis=1)
                    patch_ref[q, r * half : (r + 1) * half, (2 * a + b) * channels : (2 * a + b + 1) * channels] = (
                        piece.astype(BF16)
                    )
    wait(loads)


def index_body(owners, capacity, table_ref, pick_ref):
    targets = table_ref[...]
    slots, count = pick_ref.shape
    tall = max(owners, 16)
    hot = targets == lax.broadcasted_iota(jnp.int32, (tall, count), 0)
    sooner = lax.broadcasted_iota(jnp.int32, (count, count), 0) < lax.broadcasted_iota(
        jnp.int32, (count, count), 1
    )
    earlier = nn(jnp.where(hot, 1.0, 0.0).astype(BF16), jnp.where(sooner, 1.0, 0.0).astype(BF16))
    rank = jnp.sum(jnp.where(hot, earlier, 0.0), axis=0, keepdims=True).astype(jnp.int32)
    pick_ref[...] = jnp.where(
        targets * capacity + rank == lax.broadcasted_iota(jnp.int32, (slots, count), 0), 1.0, 0.0
    ).astype(BF16)


def pull_body(
    spaces, step,
    place, returned_ref, pick_ref, low_ref, w_hbm, w2_hbm,
    keep_ref, send_ref, high_ref, w2_ref,
    wanted, both, sems,
):
    third = low_ref.shape[0]
    parts = [(pl.ds(i * third, third), pl.ds((i - 1) * third, third)) for i in (1, 2)]
    loads = fetch([(w_hbm.at[a], high_ref.at[b]) for a, b in parts], sems)
    late = pltpu.make_async_copy(w2_hbm.at[pl.ds(0, w2_ref.shape[0])], w2_ref, sems.at[2])
    late.start()
    core = place[0] % 2
    band = both.shape[0] // spaces
    wanted[...] = (
        lax.dot_general(pick_ref[...], returned_ref[...], (((0,), (0,)), ((), ())), preferred_element_type=F32)
        .astype(BF16)
        .reshape(wanted.shape)
    )
    chips = spaces // 2
    for i in range(chips):
        both[i * band : (i + 1) * band, :] = wanted[2 * i + core]
        both[(chips + i) * band : (chips + i + 1) * band, :] = wanted[2 * i + 1 - core]
    for d in range(0, 3 * third, step):
        if d == third:
            loads[0].wait()
        if d == 2 * third:
            loads[1].wait()
        weight = low_ref[d : d + step, :] if d < third else high_ref[d - third : d - third + step, :]
        part = nt(both[...], weight).astype(BF16)
        for i in range(chips):
            keep_ref[i, :, d : d + step] = part[i * band : (i + 1) * band]
            send_ref[i, :, d : d + step] = part[(chips + i) * band : (chips + i + 1) * band]
    late.wait()


def add_body(chips, place, keep_ref, near_ref, mine_ref, *outs):
    chip = place[0] // 2
    mine_ref[...] = keep_ref[chip].astype(F32) + near_ref[chip].astype(F32)
    for j in range(1, chips):
        at = lax.rem(chip + j, chips)
        outs[j - 1][...] = (keep_ref[at].astype(F32) + near_ref[at].astype(F32)).astype(BF16)


def backward_body(rows, width, channels, hidden, block, chips, mine_ref, *rest):
    far = rest[: chips - 1]
    (
        slope_ref, n1_ref, n2_ref, inv_ref, w2_near, down_gain_ref, scale_ref, gain_ref, w1_hbm, w2_hbm,
        out_hbm, out_ref, grid, scaled, active, acc, w1_ref, w2_far, in_sems, out_sems,
    ) = rest[chips - 1 :]
    split = w2_near.shape[0]
    loads = fetch(((w2_hbm.at[pl.ds(split, hidden - split)], w2_far), (w1_hbm, w1_ref)), in_sems)
    half = width // 2
    chunks = channels // LANES
    for r in range(rows // 2):
        for a in range(2):
            for b in range(2):
                at = (pl.ds(r * half, half), pl.ds((2 * a + b) * channels, channels))
                value = mine_ref[at]
                for piece in far:
                    value = value + piece[at].astype(F32)
                for c in range(chunks):
                    grid[c, pl.ds((2 * r + a) * width + b, half, stride=2), :] = (
                        value[:, c * LANES : (c + 1) * LANES]
                    )
    gain, scale = down_gain_ref[...].reshape(1, channels), scale_ref[...].reshape(1, channels)
    for r in range(rows):
        at = pl.ds(r * width, width)
        grad = jnp.concatenate([grid[c, at, :] for c in range(chunks)], axis=1)
        back = norm_back(grad, n2_ref[at, :].astype(F32), inv_ref[at, LANES : LANES + 1], gain)
        scaled[at, :] = (back * scale).astype(BF16)
    for b in range(0, hidden, block):
        if b == split:
            loads[0].wait()
        weight = w2_near[b : b + block, :] if b < split else w2_far[b - split : b - split + block, :]
        slope = slope_ref[:, b : b + block].astype(F32)
        active[:, b : b + block] = (nt(scaled[...], weight) * slope).astype(BF16)
    loads[1].wait()
    for b in range(0, channels, block):
        acc[:, b : b + block] = nt(active[...], w1_ref[b : b + block, :])
    gain = gain_ref[...].reshape(1, channels)
    stores = []
    for r in range(rows):
        at = pl.ds(r * width, width)
        back = norm_back(acc[at, :], n1_ref[at, :].astype(F32), inv_ref[at, 0:1], gain)
        out_ref[0, r] = back.astype(BF16)
        stores.append(pltpu.make_async_copy(out_ref.at[0, r], out_hbm.at[0, r], out_sems.at[r]))
        stores[-1].start()
    wait(stores)


def push_body(chips, place, own_ref, mate_ref, pick_ref, low_ref, high_ref, out_ref, patches, tokens):
    chip, core = place[0] // 2, place[0] % 2
    band = own_ref.shape[1]
    for i in range(2 * chips):
        source_ref = own_ref if i % 2 == 0 else mate_ref
        patches[i * band : (i + 1) * band, :] = source_ref[i // 2]
    third = low_ref.shape[0]
    result = (nn(patches[:, :third], low_ref[...]) + nn(patches[:, third:], high_ref[...])).astype(BF16)
    for i in range(2 * chips):
        source = lax.rem(chip + chips - i // 2, chips)
        owner = 2 * source + (core if i % 2 == 0 else 1 - core)
        tokens[owner] = result[i * band : (i + 1) * band]
    flat = tokens[...].reshape(2 * chips * band, tokens.shape[2])
    out_ref[...] = nn(pick_ref[...], flat).astype(BF16)


def on_device(
    section_three, dw_kernel, dw_bias, mix_gain, w_expand, w_reduce, layer_scale, down_gain,
    w_down, owner_table, grad_packed,
):
    owners = lax.axis_size("dp")
    spaces = lax.axis_size("space")
    chips = spaces // 2
    slots = grad_packed.shape[1]
    capacity = slots // owners
    _, rows, width, channels = section_three.shape
    hidden = w_expand.shape[1]
    count = rows * width
    band = count // 4
    tokens = owner_table.shape[1]
    deep, narrow = w_down.shape
    place = lax.axis_index("space").astype(jnp.int32).reshape(1)
    lanes = channels // LANES
    block, step = 256, 512

    swap = [(i, i ^ 1) for i in range(spaces)]

    def send(value, pairs):
        return lax.ppermute(value, "space", pairs)

    def trade(value):
        return lax.all_to_all(value, "dp", split_axis=0, concat_axis=0, tiled=True)

    def onward(j):
        return [(i, (i + 2 * j) % spaces) for i in range(spaces)]

    (ready,) = call(prime_body, (), [], [((8, LANES), F32)], [], 1, 5e10, 1e3)
    near = send(section_three, swap)
    bands = [section_three] + [send(section_three, onward(j)) for j in range(1, chips)]
    returned = trade(grad_packed[0])

    mates = [near] + [send(bands[j], swap) for j in range(1, chips)]
    wide = chips * count
    part, w1_near, w2_whole = call(
        lambda *refs: conv_body(rows, width, channels, chips, *refs),
        (*close(dw_kernel, dw_bias, ready, *bands), *far_off(w_expand, w_reduce)),
        [VMEM] * (3 + chips) + [HBM] * 2,
        [((wide, channels), F32), (w_expand.shape, BF16), (w_reduce.shape, BF16)],
        [pltpu.VMEM((lanes, rows, width + 2 * LEFT, LANES), F32), pltpu.SemaphoreType.DMA((2,))],
        6, 4e9, 6e6,
    )
    patches, slope, n1, n2, inv, w_low = call(
        lambda *refs: forward_body(rows, width, channels, hidden, block, chips, *refs),
        (place, *close(part, dw_kernel, *mates, *bands, mix_gain, layer_scale, down_gain, w1_near, w2_whole),
         *far_off(w_down)),
        [SMEM] + [VMEM] * (7 + 2 * chips) + [HBM],
        [((chips, band, 4 * channels), BF16), ((count, hidden), BF16), ((count, channels), BF16),
         ((count, channels), BF16), ((count, 2 * LANES), F32), ((deep // 3, narrow), BF16)],
        [pltpu.VMEM((lanes, 2 * HALF, width + 2 * LEFT, LANES), F32),
         pltpu.VMEM((wide, channels), F32), pltpu.VMEM((wide, channels), BF16),
         pltpu.VMEM((wide, hidden), BF16), pltpu.VMEM((wide, channels), F32),
         pltpu.VMEM((lanes, wide, LANES), F32), pltpu.SemaphoreType.DMA((1,))],
        20, 4 * wide * channels * hidden, 9e6,
    )
    mate_patches = send(patches, swap)
    (pick,) = call(
        lambda *refs: index_body(owners, capacity, *refs),
        close(owner_table.reshape(1, tokens)), [VMEM],
        [((slots, tokens), BF16)], [], 2, 1e7, 1e5,
    )
    keep, give, w_high, w2_near = call(
        lambda *refs: pull_body(spaces, step, *refs),
        (place, *close(returned, pick, w_low), *far_off(w_down, w_reduce)),
        [SMEM] + [VMEM] * 3 + [HBM] * 2,
        [((chips, band, deep), BF16), ((chips, band, deep), BF16), ((deep - deep // 3, narrow), BF16),
         ((hidden // 3, channels), BF16)],
        [pltpu.VMEM((spaces, band, narrow), BF16), pltpu.VMEM((tokens, narrow), BF16),
         pltpu.SemaphoreType.DMA((3,))],
        6, 2 * tokens * deep * narrow, 4e6,
    )
    sent = send(give, swap)
    mine, *sums = call(
        lambda *refs: add_body(chips, *refs),
        (place, *close(keep, sent)), [SMEM, VMEM, VMEM],
        [((band, deep), F32)] + [((band, deep), BF16)] * (chips - 1), [], 4, 2e6, 1e6,
    )
    across = [send(sums[j - 1], onward(j)) for j in range(1, chips)]
    (buffer,) = call(
        lambda *refs: push_body(chips, *refs),
        (place, *close(patches, mate_patches, pick, w_low, w_high)),
        [SMEM] + [VMEM] * 5,
        [((slots, narrow), BF16)],
        [pltpu.VMEM((tokens, deep), BF16), pltpu.VMEM((spaces, band, narrow), BF16)],
        6, 2 * tokens * deep * narrow, 4e6,
    )
    arrived = trade(buffer)
    (grad_mixed,) = call(
        lambda *refs: backward_body(rows, width, channels, hidden, block, chips, *refs),
        (*close(mine, *across, slope, n1, n2, inv, w2_near, down_gain, layer_scale, mix_gain),
         *far_off(w_expand, w_reduce)),
        [VMEM] * (8 + chips) + [HBM] * 2,
        [jax.ShapeDtypeStruct(section_three.shape, BF16)],
        [pltpu.VMEM(section_three.shape, BF16), pltpu.VMEM((lanes, count, LANES), F32),
         pltpu.VMEM((count, channels), BF16), pltpu.VMEM((count, hidden), BF16),
         pltpu.VMEM((count, channels), F32),
         pltpu.VMEM(w_expand.shape, BF16), pltpu.VMEM((hidden - hidden // 3, channels), BF16),
         pltpu.SemaphoreType.DMA((2,)), pltpu.SemaphoreType.DMA((rows,))],
        16, 4 * count * channels * hidden, 9e6,
    )
    return arrived[None], grad_mixed


def solution(mesh):
    in_specs = (
        P("dp", "space", None, None), P(), P(), P(), P(), P(), P(), P(), P(None, "space"),
        P("dp", None, None), P("dp", None, "space"),
    )
    out_specs = (P("dp", None, "space"), P("dp", "space", None, None))
    return jax.shard_map(on_device, mesh=mesh, in_specs=in_specs, out_specs=out_specs, check_vma=False)
```

```python
import jax
import jax.numpy as jnp
from jax import lax
from jax.experimental import pallas as pl
from jax.experimental.pallas import tpu as pltpu
from jax.sharding import PartitionSpec as P


KS = 7
HALF = KS // 2
LANES = 128
LEFT = 8
F32 = jnp.float32
BF16 = jnp.bfloat16
VMEM = pl.BlockSpec(memory_space=pltpu.VMEM)
SMEM = pl.BlockSpec(memory_space=pltpu.SMEM)
HBM = pl.BlockSpec(memory_space=pltpu.HBM)


def far_off(*values):
    return tuple(pltpu.with_memory_space_constraint(v, pltpu.HBM) for v in values)


def close(*values):
    return tuple(pltpu.with_memory_space_constraint(v, pltpu.VMEM) for v in values)


def start(copies):
    for copy in copies:
        copy.start()


def wait(copies):
    for copy in copies:
        copy.wait()


def call(body, ins, specs, outs, scratch, limit_mib, flops, moved):
    return pl.pallas_call(
        body,
        in_specs=specs,
        out_shape=tuple(pltpu.VMEM(*o) if isinstance(o, tuple) else o for o in outs),
        out_specs=tuple(VMEM if isinstance(o, tuple) else HBM for o in outs),
        scratch_shapes=scratch,
        compiler_params=pltpu.CompilerParams(vmem_limit_bytes=limit_mib << 20),
        cost_estimate=pl.CostEstimate(
            flops=int(flops), bytes_accessed=int(moved), transcendentals=0
        ),
    )(*ins)


def nt(a, b):
    return lax.dot_general(a, b, (((1,), (1,)), ((), ())), preferred_element_type=F32)


def nn(a, b):
    return jnp.dot(a, b, preferred_element_type=F32)


def normalize(values):
    center = values - jnp.mean(values, axis=-1, keepdims=True)
    inv_std = lax.rsqrt(jnp.mean(center * center, axis=-1, keepdims=True) + 1e-06)
    return center * inv_std, inv_std


def norm_back(grad, normed, inv_std, gain):
    scaled = grad * gain
    return inv_std * (
        scaled
        - jnp.mean(scaled, axis=-1, keepdims=True)
        - normed * jnp.mean(scaled * normed, axis=-1, keepdims=True)
    )


def fetch(pairs, sems):
    copies = [pltpu.make_async_copy(src, dst, sems.at[i]) for i, (src, dst) in enumerate(pairs)]
    start(copies)
    return copies


def prime_body(out_ref):
    out_ref[...] = jnp.zeros(out_ref.shape, F32)


def convolve(padded, c, first_line, lines, total, kernel_ref, at, rows, width):
    for dx in range(KS):
        taps = [kernel_ref[dy, dx : dx + 1, at] for dy in range(KS)]
        for r in lines:
            line = padded[c, first_line(r), pl.ds(LEFT - HALF + dx, width), :]
            for out in range(rows):
                if 0 <= r - out < KS:
                    total[out] = total[out] + line * taps[r - out]
    return total


def conv_body(rows, width, channels, kernel_ref, bias_ref, ready, band_ref, *rest):
    if len(rest) > 2:
        w1_hbm, part_ref, w1_ref, padded, sems = rest
        loads = fetch(((w1_hbm, w1_ref),), sems)
    else:
        (part_ref, padded), loads = rest, []
    chunks = channels // LANES
    cols = pl.ds(LEFT, width)
    padded[:, :, 0:LEFT, :] = jnp.zeros((chunks, rows, LEFT, LANES), F32)
    padded[:, :, LEFT + width :, :] = jnp.zeros((chunks, rows, LEFT, LANES), F32)

    def own(c, _):
        at = pl.ds(pl.multiple_of(c * LANES, LANES), LANES)
        padded[c, :, cols, :] = band_ref[0, :, :, at].astype(F32)
        bias = jnp.broadcast_to(bias_ref[at].reshape(1, LANES), (width, LANES))
        lines = range(HALF, HALF + rows)
        total = convolve(padded, c, lambda r: r - HALF, lines, [bias] * rows, kernel_ref, at, rows, width)
        for out in range(rows):
            part_ref[pl.ds(out * width, width), at] = total[out]
        return 0

    lax.fori_loop(0, chunks, own, 0)
    wait(loads)


def forward_body(rows, width, channels, hidden, block, chips, place, kernel_ref, *rest):
    parts, mates, bands = rest[:chips], rest[chips : 2 * chips], rest[2 * chips : 3 * chips]
    (
        gain_ref, scale_ref, down_gain_ref, w1_ref, w2_hbm, w3_hbm,
        patch_ref, slope_ref, n1_ref, n2_ref, inv_ref, w3_ref,
        padded, mixed, first, active, acc, grid, w2_ref, sems,
    ) = rest[3 * chips :]
    pairs = ((w2_hbm, w2_ref), (w3_hbm.at[pl.ds(0, w3_ref.shape[0])], w3_ref))
    loads = [pltpu.make_async_copy(src, dst, sems.at[i]) for i, (src, dst) in enumerate(pairs)]
    loads[0].start()
    chip, odd = place[0] // 2, place[0] % 2 == 1
    chunks = channels // LANES
    count = rows * width
    cols = pl.ds(LEFT, width)
    padded[:, :, 0:LEFT, :] = jnp.zeros((chunks, 2 * HALF, LEFT, LANES), F32)
    padded[:, :, LEFT + width :, :] = jnp.zeros((chunks, 2 * HALF, LEFT, LANES), F32)
    for q in range(chips):
        level = lax.rem(chip + chips - q, chips)
        same, over, under = mates[q], mates[(q + 1) % chips], mates[(q - 1) % chips]

        def outer(c, _):
            at = pl.ds(pl.multiple_of(c * LANES, LANES), LANES)
            low, high = slice(0, HALF), slice(rows - HALF, rows)
            above = jnp.where(level > 0, over[0, high, :, at].astype(F32), 0.0)
            below = jnp.where(level < chips - 1, under[0, low, :, at].astype(F32), 0.0)
            padded[c, 0:HALF, cols, :] = jnp.where(odd, same[0, high, :, at].astype(F32), above)
            padded[c, HALF:, cols, :] = jnp.where(odd, below, same[0, low, :, at].astype(F32))
            spots = [pl.ds((q * rows + out) * width, width) for out in range(rows)]
            begun = [parts[q][pl.ds(out * width, width), at] for out in range(rows)]
            lines = [r for r in range(rows + 2 * HALF) if not HALF <= r < HALF + rows]
            total = convolve(
                padded, c, lambda r: r if r < HALF else r - rows, lines, begun,
                kernel_ref, at, rows, width,
            )
            for p, value in zip(spots, total):
                mixed[p, at] = value
            return 0

        lax.fori_loop(0, chunks, outer, 0)
    start(loads[1:])
    gain = gain_ref[...].reshape(1, channels)
    for r in range(0, chips * count, width):
        n1, inv1 = normalize(mixed[r : r + width, :])
        if r < count:
            n1_ref[r : r + width, :] = n1.astype(BF16)
            inv_ref[r : r + width, 0:LANES] = jnp.broadcast_to(inv1, (width, LANES))
        first[r : r + width, :] = (n1 * gain).astype(BF16)
    for b in range(0, hidden, block):
        pre = nn(first[...], w1_ref[:, b : b + block])
        cumulative = 0.5 * (1.0 + lax.erf(pre * 0.7071067811865476))
        mine = pre[:count]
        density = jnp.exp(-0.5 * mine * mine) * 0.3989422804014327
        slope_ref[:, b : b + block] = (cumulative[:count] + mine * density).astype(BF16)
        active[:, b : b + block] = (pre * cumulative).astype(BF16)
    loads[0].wait()
    for b in range(0, channels, block):
        acc[:, b : b + block] = nn(active[...], w2_ref[:, b : b + block])
    scale, gain = scale_ref[...].reshape(1, channels), down_gain_ref[...].reshape(1, channels)
    half = width // 2
    for q in range(chips):
        for r in range(rows):
            at = pl.ds(r * width, width)
            n2, inv2 = normalize(bands[q][0, r].astype(F32) + scale * acc[pl.ds(q * count + r * width, width), :])
            if q == 0:
                n2_ref[at, :] = n2.astype(BF16)
                inv_ref[at, LANES:] = jnp.broadcast_to(inv2, (width, LANES))
            second = n2 * gain
            for c in range(chunks):
                grid[c, pl.ds(q * count + r * width, width), :] = second[:, c * LANES : (c + 1) * LANES]
        for r in range(rows // 2):
            for a in range(2):
                for b in range(2):
                    spot = pl.ds(q * count + (2 * r + a) * width + b, half, stride=2)
                    piece = jnp.concatenate([grid[c, spot, :] for c in range(chunks)], axis=1)
                    patch_ref[q, r * half : (r + 1) * half, (2 * a + b) * channels : (2 * a + b + 1) * channels] = (
                        piece.astype(BF16)
                    )
    loads[1].wait()


def index_body(owners, capacity, table_ref, pick_ref):
    targets = table_ref[...]
    slots, count = pick_ref.shape
    tall = max(owners, 16)
    hot = targets == lax.broadcasted_iota(jnp.int32, (tall, count), 0)
    sooner = lax.broadcasted_iota(jnp.int32, (count, count), 0) < lax.broadcasted_iota(
        jnp.int32, (count, count), 1
    )
    earlier = nn(jnp.where(hot, 1.0, 0.0).astype(BF16), jnp.where(sooner, 1.0, 0.0).astype(BF16))
    rank = jnp.sum(jnp.where(hot, earlier, 0.0), axis=0, keepdims=True).astype(jnp.int32)
    pick_ref[...] = jnp.where(
        targets * capacity + rank == lax.broadcasted_iota(jnp.int32, (slots, count), 0), 1.0, 0.0
    ).astype(BF16)


def pull_body(
    spaces, step,
    place, returned_ref, pick_ref, low_ref, w_hbm, w2_hbm,
    keep_ref, send_ref, high_ref, w2_ref,
    wanted, both, sems,
):
    third = low_ref.shape[0]
    parts = [(pl.ds(i * third, third), pl.ds((i - 1) * third, third)) for i in (1, 2)]
    loads = fetch([(w_hbm.at[a], high_ref.at[b]) for a, b in parts], sems)
    late = pltpu.make_async_copy(w2_hbm.at[pl.ds(0, w2_ref.shape[0])], w2_ref, sems.at[2])
    late.start()
    core = place[0] % 2
    band = both.shape[0] // spaces
    wanted[...] = (
        lax.dot_general(pick_ref[...], returned_ref[...], (((0,), (0,)), ((), ())), preferred_element_type=F32)
        .astype(BF16)
        .reshape(wanted.shape)
    )
    chips = spaces // 2
    for i in range(chips):
        both[i * band : (i + 1) * band, :] = wanted[2 * i + core]
        both[(chips + i) * band : (chips + i + 1) * band, :] = wanted[2 * i + 1 - core]
    for d in range(0, 3 * third, step):
        if d == third:
            loads[0].wait()
        if d == 2 * third:
            loads[1].wait()
        weight = low_ref[d : d + step, :] if d < third else high_ref[d - third : d - third + step, :]
        part = nt(both[...], weight).astype(BF16)
        for i in range(chips):
            keep_ref[i, :, d : d + step] = part[i * band : (i + 1) * band]
            send_ref[i, :, d : d + step] = part[(chips + i) * band : (chips + i + 1) * band]
    late.wait()


def add_body(chips, place, keep_ref, near_ref, mine_ref, *outs):
    chip = place[0] // 2
    mine_ref[...] = keep_ref[chip].astype(F32) + near_ref[chip].astype(F32)
    for j in range(1, chips):
        at = lax.rem(chip + j, chips)
        outs[j - 1][...] = (keep_ref[at].astype(F32) + near_ref[at].astype(F32)).astype(BF16)


def backward_body(rows, width, channels, hidden, block, chips, mine_ref, *rest):
    far = rest[: chips - 1]
    (
        slope_ref, n1_ref, n2_ref, inv_ref, w2_near, down_gain_ref, scale_ref, gain_ref, w1_hbm, w2_hbm,
        out_hbm, out_ref, grid, scaled, active, acc, w1_ref, w2_far, in_sems, out_sems,
    ) = rest[chips - 1 :]
    split = w2_near.shape[0]
    loads = fetch(((w2_hbm.at[pl.ds(split, hidden - split)], w2_far), (w1_hbm, w1_ref)), in_sems)
    half = width // 2
    chunks = channels // LANES
    for r in range(rows // 2):
        for a in range(2):
            for b in range(2):
                at = (pl.ds(r * half, half), pl.ds((2 * a + b) * channels, channels))
                value = mine_ref[at]
                for piece in far:
                    value = value + piece[at].astype(F32)
                for c in range(chunks):
                    grid[c, pl.ds((2 * r + a) * width + b, half, stride=2), :] = (
                        value[:, c * LANES : (c + 1) * LANES]
                    )
    gain, scale = down_gain_ref[...].reshape(1, channels), scale_ref[...].reshape(1, channels)
    for r in range(rows):
        at = pl.ds(r * width, width)
        grad = jnp.concatenate([grid[c, at, :] for c in range(chunks)], axis=1)
        back = norm_back(grad, n2_ref[at, :].astype(F32), inv_ref[at, LANES : LANES + 1], gain)
        scaled[at, :] = (back * scale).astype(BF16)
    for b in range(0, hidden, block):
        if b == split:
            loads[0].wait()
        weight = w2_near[b : b + block, :] if b < split else w2_far[b - split : b - split + block, :]
        slope = slope_ref[:, b : b + block].astype(F32)
        active[:, b : b + block] = (nt(scaled[...], weight) * slope).astype(BF16)
    loads[1].wait()
    for b in range(0, channels, block):
        acc[:, b : b + block] = nt(active[...], w1_ref[b : b + block, :])
    gain = gain_ref[...].reshape(1, channels)
    stores = []
    for r in range(rows):
        at = pl.ds(r * width, width)
        back = norm_back(acc[at, :], n1_ref[at, :].astype(F32), inv_ref[at, 0:1], gain)
        out_ref[0, r] = back.astype(BF16)
        stores.append(pltpu.make_async_copy(out_ref.at[0, r], out_hbm.at[0, r], out_sems.at[r]))
        stores[-1].start()
    wait(stores)


def push_body(chips, place, own_ref, mate_ref, pick_ref, low_ref, high_ref, out_ref, patches, tokens):
    chip, core = place[0] // 2, place[0] % 2
    band = own_ref.shape[1]
    for i in range(2 * chips):
        source_ref = own_ref if i % 2 == 0 else mate_ref
        patches[i * band : (i + 1) * band, :] = source_ref[i // 2]
    third = low_ref.shape[0]
    result = (nn(patches[:, :third], low_ref[...]) + nn(patches[:, third:], high_ref[...])).astype(BF16)
    for i in range(2 * chips):
        source = lax.rem(chip + chips - i // 2, chips)
        owner = 2 * source + (core if i % 2 == 0 else 1 - core)
        tokens[owner] = result[i * band : (i + 1) * band]
    flat = tokens[...].reshape(2 * chips * band, tokens.shape[2])
    out_ref[...] = nn(pick_ref[...], flat).astype(BF16)


def on_device(
    section_three, dw_kernel, dw_bias, mix_gain, w_expand, w_reduce, layer_scale, down_gain,
    w_down, owner_table, grad_packed,
):
    owners = lax.axis_size("dp")
    spaces = lax.axis_size("space")
    chips = spaces // 2
    slots = grad_packed.shape[1]
    capacity = slots // owners
    _, rows, width, channels = section_three.shape
    hidden = w_expand.shape[1]
    count = rows * width
    band = count // 4
    tokens = owner_table.shape[1]
    deep, narrow = w_down.shape
    place = lax.axis_index("space").astype(jnp.int32).reshape(1)
    lanes = channels // LANES
    block, step = 256, 512

    swap = [(i, i ^ 1) for i in range(spaces)]

    def send(value, pairs):
        return lax.ppermute(value, "space", pairs)

    def trade(value):
        return lax.all_to_all(value, "dp", split_axis=0, concat_axis=0, tiled=True)

    def onward(j):
        return [(i, (i + 2 * j) % spaces) for i in range(spaces)]

    (ready,) = call(prime_body, (), [], [((8, LANES), F32)], [], 1, 5e10, 1e3)
    near = send(section_three, swap)
    bands = [section_three] + [send(section_three, onward(j)) for j in range(1, chips)]
    returned = trade(grad_packed[0])

    mates = [near] + [send(bands[j], swap) for j in range(1, chips)]
    wide = chips * count
    parts = []
    for q, value in enumerate(bands):
        parts += call(
            lambda *refs: conv_body(rows, width, channels, *refs),
            close(dw_kernel, dw_bias, ready, value) + (far_off(w_expand) if q == chips - 1 else ()),
            [VMEM] * 4 + [HBM] * (q == chips - 1),
            [((count, channels), F32)] + [(w_expand.shape, BF16)] * (q == chips - 1),
            [pltpu.VMEM((lanes, rows, width + 2 * LEFT, LANES), F32)]
            + [pltpu.SemaphoreType.DMA((1,))] * (q == chips - 1),
            4, 2e9, 2e6,
        )
    w1_near = parts.pop()
    patches, slope, n1, n2, inv, w_low = call(
        lambda *refs: forward_body(rows, width, channels, hidden, block, chips, *refs),
        (place, *close(dw_kernel, *parts, *mates, *bands, mix_gain, layer_scale, down_gain, w1_near),
         *far_off(w_reduce, w_down)),
        [SMEM] + [VMEM] * (5 + 3 * chips) + [HBM] * 2,
        [((chips, band, 4 * channels), BF16), ((count, hidden), BF16), ((count, channels), BF16),
         ((count, channels), BF16), ((count, 2 * LANES), F32), ((deep // 3, narrow), BF16)],
        [pltpu.VMEM((lanes, 2 * HALF, width + 2 * LEFT, LANES), F32),
         pltpu.VMEM((wide, channels), F32), pltpu.VMEM((wide, channels), BF16),
         pltpu.VMEM((wide, hidden), BF16), pltpu.VMEM((wide, channels), F32),
         pltpu.VMEM((lanes, wide, LANES), F32),
         pltpu.VMEM(w_reduce.shape, BF16), pltpu.SemaphoreType.DMA((2,))],
        20, 4 * wide * channels * hidden, 9e6,
    )
    mate_patches = send(patches, swap)
    (pick,) = call(
        lambda *refs: index_body(owners, capacity, *refs),
        close(owner_table.reshape(1, tokens)), [VMEM],
        [((slots, tokens), BF16)], [], 2, 1e7, 1e5,
    )
    keep, give, w_high, w2_near = call(
        lambda *refs: pull_body(spaces, step, *refs),
        (place, *close(returned, pick, w_low), *far_off(w_down, w_reduce)),
        [SMEM] + [VMEM] * 3 + [HBM] * 2,
        [((chips, band, deep), BF16), ((chips, band, deep), BF16), ((deep - deep // 3, narrow), BF16),
         ((hidden // 3, channels), BF16)],
        [pltpu.VMEM((spaces, band, narrow), BF16), pltpu.VMEM((tokens, narrow), BF16),
         pltpu.SemaphoreType.DMA((3,))],
        6, 2 * tokens * deep * narrow, 4e6,
    )
    sent = send(give, swap)
    mine, *sums = call(
        lambda *refs: add_body(chips, *refs),
        (place, *close(keep, sent)), [SMEM, VMEM, VMEM],
        [((band, deep), F32)] + [((band, deep), BF16)] * (chips - 1), [], 4, 2e6, 1e6,
    )
    across = [send(sums[j - 1], onward(j)) for j in range(1, chips)]
    (buffer,) = call(
        lambda *refs: push_body(chips, *refs),
        (place, *close(patches, mate_patches, pick, w_low, w_high)),
        [SMEM] + [VMEM] * 5,
        [((slots, narrow), BF16)],
        [pltpu.VMEM((tokens, deep), BF16), pltpu.VMEM((spaces, band, narrow), BF16)],
        6, 2 * tokens * deep * narrow, 4e6,
    )
    arrived = trade(buffer)
    (grad_mixed,) = call(
        lambda *refs: backward_body(rows, width, channels, hidden, block, chips, *refs),
        (*close(mine, *across, slope, n1, n2, inv, w2_near, down_gain, layer_scale, mix_gain),
         *far_off(w_expand, w_reduce)),
        [VMEM] * (8 + chips) + [HBM] * 2,
        [jax.ShapeDtypeStruct(section_three.shape, BF16)],
        [pltpu.VMEM(section_three.shape, BF16), pltpu.VMEM((lanes, count, LANES), F32),
         pltpu.VMEM((count, channels), BF16), pltpu.VMEM((count, hidden), BF16),
         pltpu.VMEM((count, channels), F32),
         pltpu.VMEM(w_expand.shape, BF16), pltpu.VMEM((hidden - hidden // 3, channels), BF16),
         pltpu.SemaphoreType.DMA((2,)), pltpu.SemaphoreType.DMA((rows,))],
        16, 4 * count * channels * hidden, 9e6,
    )
    return arrived[None], grad_mixed


def solution(mesh):
    in_specs = (
        P("dp", "space", None, None), P(), P(), P(), P(), P(), P(), P(), P(None, "space"),
        P("dp", None, None), P("dp", None, "space"),
    )
    out_specs = (P("dp", None, "space"), P("dp", "space", None, None))
    return jax.shard_map(on_device, mesh=mesh, in_specs=in_specs, out_specs=out_specs, check_vma=False)
```
